32 devices in a mesh: strip: 4 (over z), date: 8 (over y, x, core).
Axes of the slice: x: 2, y: 2, z: 4, core: 2. Of those that a mesh axis runs over, the one named last changes fastest.
Arguments:
- images: bfloat16 [128, 256, 128], P('date', 'strip'), may hold values from 0.19921875 to 5
- inverse_blocks: float32 [2, 8, 128, 128], P(None, 'strip', 'date'), as said below
- pair_first: int32 [256], P('date'), may hold values from 0 to 15
- pair_block: int32 [256, 1], P('date'), may hold values from 0 to 7; in each aligned block of 32 rows (0 to 31, 32 to 63, ...) at most 8 rows name the same one
- pair_second: int32 [256], P('date'), may hold values from 0 to 15
- pair_count: int32 [8], P('date'), may hold values from 8 to 32, as said below
- shifts: int32 [256, 2, 8], P('date', None, 'strip'), may hold values from -8 to 8
- anchors: int32 [8], P('strip'), may hold values from 0 to 96, as said below
Outputs:
- pair_offsets: float32 [256, 2, 8], P('date', None, 'strip')
- series: float32 [2, 8, 128], P(None, 'strip', 'date')
The draws below stay inside these ranges and needn't reach their ends.
Inputs may be any that keep to these rules, and one draw needn't show every extreme that they name: `pair_block`: among the 32 slots of one date block at most 8 name one partner block, and some block is named that often. `pair_count`: slots 0 to count - 1 of a date block are live; slots at or past the count carry no pair, and their partner windows need not be sent. One block has all 32 live, one has 8, every other block 24 or more. `anchors`: chip q starts at column (q % 2) * 64 plus 0 to 32. `inverse_blocks`: symmetric in its last two dimensions.
All inputs are finite; a program needn't handle non-finite values.
Results may differ from the reference program's by a relative error of at most 0.008.
Values may be sent and summed in bfloat16 or wider, within the bound.
A program may use at most 64 MiB of HBM per device.

```python
import math
import jax
import jax.numpy as jnp
import numpy as np
from jax import lax

CHIP = 64
SMAX = 8
DATE_DEV = 16
NCHIP = 2
PAIR_DEV = 32
CAP = 8
BLOCKS = 8
NDATE = 128
PAIRS = 256
COLS = 128
BAND_ROWS = 256
CHIPS_ALL = 8


def draw_inverse_blocks(key, part):
    subkeys = jax.random.split(key, 2)
    noise_part = jax.random.normal(subkeys[0], (2, CHIPS_ALL, NDATE, NDATE), jnp.float32) * (0.5 / math.sqrt(NDATE))
    mirror = (noise_part + jnp.swapaxes(noise_part, 2, 3)) * (1.0 / math.sqrt(2.0))
    diag_vals = jnp.exp(jax.random.uniform(subkeys[1], (2, CHIPS_ALL, NDATE), jnp.float32, math.log(0.5), math.log(2.0)))
    result = mirror + diag_vals[..., None] * jnp.eye(NDATE, dtype=jnp.float32)
    return result


def draw_pair_count(key, part):
    subkeys = jax.random.split(key, 2)
    counts = jax.random.randint(subkeys[0], (BLOCKS,), 3 * PAIR_DEV // 4, PAIR_DEV + 1, jnp.int32)
    shuffled = jax.random.permutation(subkeys[1], BLOCKS)
    counts = counts.at[shuffled[0]].set(PAIR_DEV)
    counts = counts.at[shuffled[1]].set(PAIR_DEV // 4)
    return counts


def draw_anchors(key, part):
    chip_ids = jnp.arange(CHIPS_ALL, dtype=jnp.int32)
    offsets_in = jax.random.randint(key, (CHIPS_ALL,), 0, CHIP // 2 + 1, jnp.int32)
    offsets_in = offsets_in.at[0].set(0)
    offsets_in = offsets_in.at[CHIPS_ALL - 1].set(CHIP // 2)
    return chip_ids % NCHIP * CHIP + offsets_in


def touch_ends(entries, rng, least, largest):
    extent = entries.shape
    place = [jax.random.randint(jax.random.fold_in(rng, axis), (), 0, extent[axis]) for axis in range(len(extent))]
    entries = entries.at[tuple(place)].set(least)
    longest = extent.index(max(extent))
    place[longest] = (place[longest] + 1) % extent[longest]
    return entries.at[tuple(place)].set(largest)


def shard_levels(own_key, shape, pieces, low, top_value):
    loudness, own = 1.0, jax.random.fold_in(own_key, 6)
    for axis_at, shards_of in pieces:
        heights = jnp.exp(jax.random.uniform(jax.random.fold_in(own, axis_at), (shards_of,), jnp.float32, low / len(pieces), top_value / len(pieces)))
        loudness = loudness * jnp.repeat(heights, shape[axis_at] // shards_of).reshape([-1 if axis == axis_at else 1 for axis in range(len(shape))])
    return loudness


def routed_block(stream_key, own, number, rows, amount, top, limit, lean):
    sequence = jax.random.permutation(stream_key, amount)
    packed, usual = shares(amount, rows * top, limit, lean, True), shares(amount, rows * top, limit, lean, False)
    places = jnp.arange(amount)

    def named(tallies, turn):
        used = int((tallies > 0).sum())
        fixed = max(1, used // 4)
        moved = fixed + (places - fixed + turn * (used - fixed)) % max(1, amount - fixed)
        return jnp.zeros((amount,), jnp.int32).at[sequence[jnp.where(places < fixed, places, moved)]].set(jnp.asarray(tallies, jnp.int32))

    tallies = jnp.where(number % 4 == 0, named(packed, number // 4), named(usual, number - number // 4 - 1))
    mixed = jax.random.permutation(jax.random.fold_in(own, 3), amount)
    giver, sink = mixed[0:amount // 2 * 2:2], mixed[1:amount // 2 * 2:2]
    room = jnp.minimum(tallies[giver] - 1, limit - tallies[sink]) // 2
    room = jnp.where((giver == sequence[0]) | (sink == sequence[0]) | (tallies[sink] == 0), 0, jnp.maximum(room, 0))
    moved = jax.random.randint(jax.random.fold_in(own, 4), (amount // 2,), 0, 1 << 20) % (room + 1)
    tallies = tallies.at[giver].add(-moved).at[sink].add(moved)
    items = jnp.searchsorted(jnp.cumsum(tallies), jnp.arange(rows * top), side="right").astype(jnp.int32)
    grid = items.reshape(top, rows).T
    grid = grid[jax.random.permutation(jax.random.fold_in(own, 1), rows)]
    turn = jax.random.randint(jax.random.fold_in(own, 2), (rows, 1), 0, top)
    return jnp.take_along_axis(grid, (jnp.arange(top)[None, :] + turn) % top, axis=1)


def shares(count, total, limit, lean, full):
    portions = [(1 << 20) // math.isqrt(grade ** lean) + 1 for grade in range(1, count + 1)]
    largest = limit if full else min(limit, max(-(-total // count), total * portions[0] // sum(portions)))
    least = 1 if total - largest >= count - 1 else 0
    given, rest = [largest] + [least] * (count - 1), total - largest - least * (count - 1)
    while rest > 0:
        free = [i for i in range(1, count) if given[i] < largest] or [i for i in range(1, count) if given[i] < limit]
        pool, left = sum([portions[i] for i in free]), rest
        for i in free:
            extra = min(limit - given[i], max(1, left * portions[i] // pool), rest)
            given[i] = given[i] + extra
            rest = rest - extra
    return np.array(given)


def setup_inputs(seed: int = 0) -> dict:
    streams_of = jax.random.split(jax.random.key(seed), 9)
    images = jnp.clip(jnp.exp(math.log(5.0) - 3.2227897 * jax.random.uniform(streams_of[0], (NDATE, BAND_ROWS, COLS), jnp.float32) ** shard_levels(streams_of[0], (NDATE, BAND_ROWS, COLS), ((0, 8), (1, 4)), -0.2, 0.2)), 0.19921875, 5.0).astype(jnp.bfloat16)
    inverse_blocks = draw_inverse_blocks(jax.random.fold_in(streams_of[8], 71), 0)
    pair_first = touch_ends(jax.random.randint(streams_of[2], (PAIRS,), 0, DATE_DEV), jax.random.fold_in(streams_of[2], 1), 0, DATE_DEV - 1).astype(jnp.int32)
    pair_block_keys = jax.random.split(jax.random.fold_in(streams_of[3], 1), PAIRS // PAIR_DEV)
    pair_block_turns = jax.random.permutation(jax.random.fold_in(streams_of[3], 3), PAIRS // PAIR_DEV)
    pair_block = jax.vmap(lambda own, number: routed_block(jax.random.fold_in(streams_of[3], 2), own, number, PAIR_DEV, BLOCKS, 1, CAP, 1))(pair_block_keys, pair_block_turns).reshape((PAIRS, 1))
    pair_second = touch_ends(jax.random.randint(streams_of[4], (PAIRS,), 0, DATE_DEV), jax.random.fold_in(streams_of[4], 1), 0, DATE_DEV - 1).astype(jnp.int32)
    pair_count = draw_pair_count(jax.random.fold_in(streams_of[8], 71), 0)
    shifts = touch_ends(jax.random.randint(streams_of[6], (PAIRS, 2, CHIPS_ALL), -SMAX, SMAX + 1), jax.random.fold_in(streams_of[6], 1), -SMAX, SMAX).astype(jnp.int32)
    anchors = draw_anchors(jax.random.fold_in(streams_of[8], 71), 0)
    return {"images": images, "inverse_blocks": inverse_blocks, "pair_first": pair_first, "pair_block": pair_block, "pair_second": pair_second, "pair_count": pair_count, "shifts": shifts, "anchors": anchors}


def make_tables(length):
    counter = jnp.arange(length, dtype=jnp.int32)
    products = (counter[:, None] * counter[None, :]) % length
    radians = products.astype(jnp.float32) * (2.0 * math.pi / length)
    cosine = jnp.cos(radians)
    sine_part = -jnp.sin(radians)
    forward = jnp.concatenate([cosine, sine_part], axis=1).astype(jnp.bfloat16)
    over_len = 2 * length
    signed = jnp.where(counter < length // 2, counter, counter - length)
    places = jnp.arange(over_len, dtype=jnp.int32)
    turned = (signed[:, None] * places[None, :]) % over_len
    angles = turned.astype(jnp.float32) * (2.0 * math.pi / over_len)
    vcosine = jnp.cos(angles)
    vsine = jnp.sin(angles)
    top_rows = jnp.concatenate([vcosine, vsine], axis=1)
    low_rows = jnp.concatenate([-vsine, vcosine], axis=1)
    inverse_rows = jnp.concatenate([top_rows, low_rows], axis=0).astype(jnp.bfloat16)
    displace = (((places + length) % over_len) - length).astype(jnp.float32) * 0.5
    return (forward, cosine.astype(jnp.bfloat16), sine_part.astype(jnp.bfloat16), inverse_rows,
            vcosine.T.astype(jnp.bfloat16), vsine.T.astype(jnp.bfloat16), displace)


def product(form, left, right):
    return jnp.einsum(form, left.astype(jnp.float32), right.astype(jnp.float32), precision=lax.Precision.HIGHEST)


def spectra(windows, tables):
    forward, cosine_b, sine_b = tables[0], tables[1], tables[2]
    length = windows.shape[-1]
    values = windows.astype(jnp.float32)
    centred = (values - jnp.mean(values, axis=(1, 2), keepdims=True)).astype(jnp.bfloat16)
    section_one = product("bmn,nk->bmk", centred, forward).astype(jnp.bfloat16)
    with_cos = product("km,bmj->bkj", cosine_b, section_one)
    with_sin = product("km,bmj->bkj", sine_b, section_one)
    real_part = with_cos[:, :, :length] - with_sin[:, :, length:]
    imag_part = with_sin[:, :, :length] + with_cos[:, :, length:]
    return jnp.concatenate([real_part, imag_part], axis=2).astype(jnp.bfloat16)


def centroid(near_spec, far_spec, tables):
    inverse_rows, back_cos, back_sin, displace = tables[3], tables[4], tables[5], tables[6]
    length = near_spec.shape[-1] // 2
    near_re = near_spec[:, :, :length].astype(jnp.float32)
    near_im = near_spec[:, :, length:].astype(jnp.float32)
    far_re = far_spec[:, :, :length].astype(jnp.float32)
    far_im = far_spec[:, :, length:].astype(jnp.float32)
    cross_re = near_re * far_re + near_im * far_im
    cross_im = near_im * far_re - near_re * far_im
    cross_spec = jnp.concatenate([cross_re, cross_im], axis=2).astype(jnp.bfloat16)
    along = product("bun,nl->bul", cross_spec, inverse_rows).astype(jnp.bfloat16)
    half_width = along.shape[-1] // 2
    surface = product("ku,bul->bkl", back_cos, along[:, :, :half_width]) - product("ku,bul->bkl", back_sin, along[:, :, half_width:])
    energy = surface * surface
    norm_val = jnp.mean(energy, axis=(1, 2)) + 1e-6
    row_shift = jnp.mean(energy * displace[None, :, None], axis=(1, 2)) / norm_val
    col_shift = jnp.mean(energy * displace[None, None, :], axis=(1, 2)) / norm_val
    return jnp.stack([row_shift, col_shift], axis=1)


def reference(images, inverse_blocks, pair_first, pair_block, pair_second, pair_count, shifts, anchors):
    length = CHIP
    margin = SMAX
    tables = make_tables(length)
    padded = jnp.pad(images, ((0, 0), (margin, margin), (margin, margin + length // 2)))
    chip_ids = jnp.arange(CHIPS_ALL, dtype=jnp.int32)
    row_base = ((chip_ids // NCHIP) * length + margin).astype(jnp.int32)
    col_base = (anchors + margin).astype(jnp.int32)

    def cut_window(image_rows, row_at, col_at):
        return lax.dynamic_slice(image_rows, (row_at, col_at), (length, length))

    def one_pair(slot):
        block_id = slot // PAIR_DEV
        first_id = (block_id * DATE_DEV + pair_first[slot]).astype(jnp.int32)
        second_id = (pair_block[slot, 0] * DATE_DEV + pair_second[slot]).astype(jnp.int32)
        live_mask = ((slot % PAIR_DEV) < pair_count[block_id]).astype(jnp.float32)
        near_img = lax.dynamic_index_in_dim(padded, first_id, 0, keepdims=False)
        far_img = lax.dynamic_index_in_dim(padded, second_id, 0, keepdims=False)
        near_win = jax.vmap(cut_window, in_axes=(None, 0, 0))(near_img, row_base, col_base)
        far_win = jax.vmap(cut_window, in_axes=(None, 0, 0))(far_img, (row_base + shifts[slot, 0]).astype(jnp.int32), (col_base + shifts[slot, 1]).astype(jnp.int32))
        found = centroid(spectra(near_win, tables), spectra(far_win, tables), tables)
        return (shifts[slot].astype(jnp.float32) + found.T) * live_mask

    pair_offsets = lax.map(one_pair, jnp.arange(PAIRS, dtype=jnp.int32))
    slot_ids = jnp.arange(PAIRS, dtype=jnp.int32)
    first_all = ((slot_ids // PAIR_DEV) * DATE_DEV + pair_first).astype(jnp.int32)
    second_all = (pair_block[:, 0] * DATE_DEV + pair_second).astype(jnp.int32)
    rhs_all = jax.ops.segment_sum(pair_offsets, second_all, num_segments=NDATE) - jax.ops.segment_sum(pair_offsets, first_all, num_segments=NDATE)
    rhs_all = jnp.transpose(rhs_all, (1, 2, 0))
    series = jnp.einsum("xqde,xqe->xqd", inverse_blocks, rhs_all, precision=lax.Precision.HIGHEST)
    return (pair_offsets, series)
```

```python
import functools
import math

import jax
import jax.numpy as jnp
import numpy as np
from jax import lax
from jax.experimental import pallas as pl
from jax.experimental.pallas import tpu as pltpu
from jax.sharding import PartitionSpec as P

SMAX = 8
MESH = pl.DeviceIdType.MESH
F32, BF16, I32 = jnp.float32, jnp.bfloat16, jnp.int32


def make_tables(length):
    counter = np.arange(length)
    radians = (counter[:, None] * counter[None, :] % length) * (2.0 * math.pi / length)
    cosine, sine = np.cos(radians), -np.sin(radians)
    over = 2 * length
    signed = np.where(counter < length // 2, counter, counter - length)
    places = np.arange(over)
    angles = (signed[:, None] * places[None, :] % over) * (2.0 * math.pi / over)
    vcos, vsin = np.cos(angles), np.sin(angles)
    forward = np.concatenate([cosine, sine, -sine, cosine], axis=1)
    forward = np.concatenate([forward, np.zeros_like(forward)], axis=0)
    rows = np.concatenate([cosine, sine], axis=1)
    one = np.concatenate([vcos, vsin], axis=1)
    two = np.concatenate([-vsin, vcos], axis=1)
    back = np.concatenate([one, one, two, -two], axis=0)
    final = np.concatenate([vcos.T, -vsin.T], axis=1)
    return [jnp.asarray(t.astype(np.float32)).astype(BF16) for t in (forward, rows, back, final)]


def remote(k, src, dst, where, send, recv):
    return pltpu.make_async_remote_copy(
        src_ref=src,
        dst_ref=dst,
        send_sem=send.at[k],
        recv_sem=recv.at[k],
        device_id=where,
        device_id_type=MESH,
    )


class Gather:
    def __init__(self, me, strip, strips, blocks, send, recv):
        self.blocks = blocks
        groups = blocks[0].shape[0]
        half = (groups - 2) // 2
        last = groups - 2
        self.has_up, self.has_down = strip > 0, strip < strips - 1
        up, down = lax.max(strip - 1, 0), lax.min(strip + 1, strips - 1)
        to = {j: jnp.bitwise_xor(me, j) for j in (1, 2, 4)}
        self.to, self.up, self.down = to, up, down
        self.copies = {}
        self.kinds = 0

        def add(name, d, at, many, where, target, dst_at=None):
            dst_at = at if dst_at is None else dst_at
            copy = remote(
                self.kinds,
                blocks[d].at[pl.ds(at, many)],
                blocks[target].at[pl.ds(dst_at, many)],
                where,
                send,
                recv,
            )
            self.copies[name] = copy
            self.kinds += 1

        one, two = (1, half), (1 + half, half)
        one_edge, one_rest = (1, 1), (2, half - 1)
        two_edge, two_rest = (last, 1), (1 + half, half - 1)
        for link, first, edge, rest, relayed, r_edge, r_rest in (
            (4, one, two_edge, two_rest, 2, two_edge, two_rest),
            (2, two, one_edge, one_rest, 4, one_edge, one_rest),
        ):
            where = {"date": to[link]}
            add((link, "first"), 0, *first, where, link)
            add((link, "edge"), 0, *edge, where, link)
            add((link, "rest"), 0, *rest, where, link)
            add((link, "relay_edge"), relayed, *r_edge, where, 6)
            add((link, "relay_rest"), relayed, *r_rest, where, 6)
        where = {"date": to[1]}
        add("core", 0, 1, 2 * half, where, 1)
        for d in (2, 4, 6):
            add(("core", d, "one"), d, *one, where, d ^ 1)
            add(("core", d, "two"), d, *two, where, d ^ 1)
        for d in (0, 2, 4, 6):
            for flip in (0, 1):
                spot = {"date": jnp.bitwise_xor(me, flip)} if flip else {}
                add(("up", d, flip), d, 1, 1, {"strip": up, **spot}, d ^ flip, groups - 1)
                add(("down", d, flip), d, last, 1, {"strip": down, **spot}, d ^ flip, 0)

    def start(self, *names):
        for name in names:
            self.copies[name].start()

    def got(self, *names):
        for name in names:
            self.copies[name].wait_recv()

    def z_start(self, side, d):
        has = self.has_up if side == "up" else self.has_down

        @pl.when(has)
        def _():
            for flip in (0, 1):
                self.copies[(side, d, flip)].start()

    def z_got(self, d, flips=(0, 1)):
        @pl.when(self.has_down)
        def _():
            for flip in flips:
                self.copies[("up", d, flip)].wait_recv()

        @pl.when(self.has_up)
        def _():
            for flip in flips:
                self.copies[("down", d, flip)].wait_recv()

    def left(self):
        for name, copy in self.copies.items():
            if name[0] == "up":
                pl.when(self.has_up)(copy.wait_send)
            elif name[0] == "down":
                pl.when(self.has_down)(copy.wait_send)
            else:
                copy.wait_send()


def plain_gather(n, me, strip, strips, grid, send, recv):
    groups = grid.shape[1]
    has_up, has_down = strip > 0, strip < strips - 1
    up, down = lax.max(strip - 1, 0), lax.min(strip + 1, strips - 1)
    z_up = remote(0, grid.at[me, 1], grid.at[me, groups - 1], {"strip": up}, send, recv)
    z_down = remote(1, grid.at[me, groups - 2], grid.at[me, 0], {"strip": down}, send, recv)
    pl.when(has_up)(z_up.start)
    pl.when(has_down)(z_down.start)
    copies = []
    peers = [{"date": lax.rem(me + j, n)} for j in range(1, n)]
    main = pl.ds(1, groups - 2)
    for j, peer in enumerate(peers):
        part = grid.at[me, main]
        copies.append(remote(2 + j, part, part, peer, send, recv))
        copies[-1].start()
    pl.when(has_down)(z_up.wait_recv)
    pl.when(has_up)(z_down.wait_recv)
    pl.when(has_up)(z_up.wait_send)
    pl.when(has_down)(z_down.wait_send)
    for side, at in ((0, 0), (1, groups - 1)):
        for j, peer in enumerate(peers):
            part = grid.at[me, at]
            copies.append(remote(2 + (1 + side) * (n - 1) + j, part, part, peer, send, recv))
            copies[-1].start()
    for copy in copies:
        copy.wait()


def pairs_kernel(
    n, strips, cap,
    first_h, block_h, second_h, count_h, shifts_h, anchors_h,
    img, inverse_h, forward_h, rows_h, back_h, final_h,
    offsets_out, series_out,
    first_s, block_s, second_s, count_s, shifts_s, anchors_s, perm_s,
    first_v, block_v, second_v, shifts_v, inverse, forward, rows, back, final,
    grid, late_a, late_b, partial, held_sums,
    local, send, recv,
    wide, far, near, spec, sums, moments, picked, spread_v, columns_v, perm_v,
):
    groups, dates, _, cols = grid.shape[1:]
    length = SMAX * (groups - 2)
    pairs, chips = first_s.shape[1], anchors_s.shape[0]
    fast = n == 8
    me, strip = lax.axis_index("date"), lax.axis_index("strip")
    has_up, has_down = strip > 0, strip < strips - 1
    up, down = lax.max(strip - 1, 0), lax.min(strip + 1, strips - 1)

    barrier = pltpu.get_barrier_semaphore()
    if fast:
        greeted = [{"date": jnp.bitwise_xor(me, j)} for j in (1, 2, 4)]
        side_spots = [{}, {"date": jnp.bitwise_xor(me, 1)}]
    else:
        greeted = [{"date": lax.rem(me + j, n)} for j in range(1, n)]
        side_spots = [{}]
    for where in greeted:
        pl.semaphore_signal(barrier, inc=1, device_id=where, device_id_type=MESH)
    for other, has in ((up, has_up), (down, has_down)):
        @pl.when(has)
        def _():
            for spot in side_spots:
                pl.semaphore_signal(
                    barrier, inc=1, device_id={"strip": other, **spot}, device_id_type=MESH
                )

    count = iter(range(local.shape[0]))

    def load(src, dst):
        copy = pltpu.make_async_copy(src, dst, local.at[next(count)])
        copy.start()
        return copy

    own = 0 if fast else me
    mine = [load(img.at[:, g], grid.at[own, 1 + g]) for g in range(groups - 2)]
    small = [
        load(a, b)
        for a, b in (
            (first_h, first_s), (block_h, block_s), (second_h, second_s), (count_h, count_s),
            (shifts_h, shifts_s), (anchors_h, anchors_s),
            (first_h, first_v), (block_h, block_v), (second_h, second_v), (shifts_h, shifts_v),
        )
    ]
    large = [
        load(a, b)
        for a, b in (
            (forward_h, forward), (rows_h, rows), (back_h, back), (final_h, final),
            (inverse_h, inverse),
        )
    ]
    sides = len(side_spots) * (has_up.astype(I32) + has_down.astype(I32))
    pl.semaphore_wait(barrier, len(greeted) + sides)
    for copy in mine:
        copy.wait()
    if fast:
        blocks = [grid.at[d] for d in range(6)] + [late_a, late_b]
        move = Gather(me, strip, strips, blocks, send, recv)
        move.start((4, "first"), (2, "first"))
        move.z_start("up", 0)
        move.z_start("down", 0)
        move.start((4, "edge"), (2, "edge"), (4, "rest"), (2, "rest"), "core")
    for copy in small + large:
        copy.wait()

    line = lax.broadcasted_iota(I32, (pairs, pairs), 0)
    place = lax.broadcasted_iota(I32, (pairs, pairs), 1)
    if fast:
        distance = jnp.bitwise_xor(block_v[...], me)
        key = jnp.broadcast_to(jnp.maximum(distance - 5, 0), (pairs, pairs))
        key_line = jnp.sum(jnp.where(line == place, key, 0), axis=1, keepdims=True)
        ahead = (key < key_line) | ((key == key_line) & (place < line))
        rank_line = jnp.sum(ahead.astype(I32), axis=1, keepdims=True)
        behind = (key_line < key) | ((key_line == key) & (line < place))
        rank = jnp.sum(behind.astype(I32), axis=0, keepdims=True)
        perm_v[...] = jnp.sum(jnp.where(rank_line == place, line, 0), axis=0, keepdims=True)
        ordered = load(perm_v, perm_s)
        pick = (jnp.broadcast_to(rank, (pairs, pairs)) == line).astype(F32)
    else:
        pick = (line == place).astype(F32)
    picked[...] = pick

    def chosen(row):
        return jnp.sum(pick * row, axis=1, keepdims=True)

    spot = lax.broadcasted_iota(I32, (pairs, partial.shape[1]), 1).astype(F32)
    to_date = chosen((block_v[...] * dates + second_v[...]).astype(F32))
    from_date = chosen((me * dates + first_v[...]).astype(F32))
    spread_v[...] = (spot == to_date).astype(F32) - (spot == from_date).astype(F32)
    live = (lax.broadcasted_iota(I32, (1, pairs), 1) < count_s[0]).astype(F32)
    at = lax.broadcasted_iota(I32, columns_v.shape, 1)
    held_columns = jnp.where(at == 2 * chips, chosen(live), 0.0)
    for x in range(2):
        for c in range(chips):
            column = chosen(shifts_v[x, c:c + 1].astype(F32))
            held_columns = jnp.where(at == x * chips + c, column, held_columns)
    columns_v[...] = held_columns

    lane = lax.broadcasted_iota(I32, (length, cols), 1)

    def turned(value, start):
        rolled = pltpu.roll(value, lax.rem(2 * cols - start, cols), 1)
        inside = (lane >= -start) & (lane < cols - start)
        return jnp.where(inside, rolled, 0.0).astype(BF16)

    width = 2 * length
    lanes2 = lax.broadcasted_iota(I32, (1, 2 * width), 1)
    base = jnp.where((lanes2 == 0) | (lanes2 == width + length), 1.0 / length, 0.0)

    def spectra(ref, at, many):
        windows = ref[pl.ds(at, many)].reshape(many * length, cols)
        section = jnp.dot(windows, forward[...], preferred_element_type=F32)
        stacked = []
        for w in range(many):
            part = section[w * length:(w + 1) * length]
            part = (part - jnp.sum(part, axis=0, keepdims=True) * base).astype(BF16)
            stacked.append(jnp.concatenate([part[:, :width], part[:, width:]], axis=0))
        return jnp.dot(
            rows[...], jnp.concatenate(stacked, axis=1), preferred_element_type=F32
        )

    def near_part(low, high):
        for d in range(low, high):
            value = grid[own, pl.ds(1, groups - 2), d].astype(F32).reshape(length, cols)
            for c in range(chips):
                near[d * chips + c] = turned(value, anchors_s[c])
        many = (high - low) * chips
        found = spectra(near, low * chips, many)
        for w in range(many):
            value = found[:, w * width:(w + 1) * width]
            both = jnp.concatenate([value, pltpu.roll(value, length, 1)], axis=1)
            spec[low * chips + w] = both.astype(BF16)

    def far_cut(i, stage):
        p = perm_s[0, i] if fast else i
        block, day = block_s[0, p], second_s[0, p]
        if fast:
            distance = jnp.bitwise_xor(block, me)
            value = grid[jnp.where(distance < 6, distance, 0), :, day].astype(F32)
            if stage > 1:
                value = jnp.where(distance == 6, late_a[:, day].astype(F32), value)
            if stage > 2:
                value = jnp.where(distance == 7, late_b[:, day].astype(F32), value)
        else:
            value = grid[block, :, day].astype(F32)
        wide[i, pl.ds(0, SMAX)] = jnp.where(has_up, value[0], 0.0)
        wide[i, pl.ds(SMAX, length)] = value[1:groups - 1].reshape(length, cols)
        wide[i, pl.ds(SMAX + length, SMAX)] = jnp.where(has_down, value[groups - 1], 0.0)
        for c in range(chips):
            window = wide[i, pl.ds(SMAX + shifts_s[0, c, p], length)]
            far[i * chips + c] = turned(window, anchors_s[c] + shifts_s[1, c, p])
        return first_s[0, p]

    steps = lax.broadcasted_iota(I32, (width, 1), 0)
    down_k = jnp.where(steps < length, steps, steps - width).astype(F32) * 0.5
    down_k = jnp.broadcast_to(down_k, (width, width))

    def far_part(low, high, stage):
        days = [far_cut(i, stage) for i in range(low, high)]
        many = (high - low) * chips
        found = spectra(far, low * chips, many).astype(BF16)
        crossed = []
        for b, day in enumerate(days):
            for c in range(chips):
                w = b * chips + c
                value = found[:, w * width:(w + 1) * width]
                crossed.append(spec[day * chips + c] * jnp.concatenate([value, value], axis=1))
        along = jnp.dot(
            jnp.concatenate(crossed, axis=0), back[...], preferred_element_type=F32
        ).astype(BF16)
        stacked = []
        for w in range(many):
            part = along[w * length:(w + 1) * length]
            stacked.append(jnp.concatenate([part[:, :width], part[:, width:]], axis=0))
        surface = jnp.dot(
            final[...], jnp.concatenate(stacked, axis=1), preferred_element_type=F32
        )
        for b in range(high - low):
            for c in range(chips):
                w = b * chips + c
                value = surface[:, w * width:(w + 1) * width]
                energy = value * value
                at = (c, pl.ds(low + b, 1))
                sums[at] = jnp.sum(energy, axis=0, keepdims=True)
                moments[at] = jnp.sum(energy * down_k, axis=0, keepdims=True)

    middle = dates // 2
    if fast:
        near_part(0, middle)
        move.got((2, "first"))
        move.start((4, "relay_edge"))
        move.z_start("down", 2)
        move.got((4, "first"))
        move.start((2, "relay_edge"))
        move.z_start("up", 4)
        move.start((4, "relay_rest"), (2, "relay_rest"), ("core", 2, "two"), ("core", 4, "one"))
        near_part(middle, dates)
        move.got((2, "edge"))
        move.z_start("up", 2)
        move.got((4, "edge"))
        move.z_start("down", 4)
        ordered.wait()
        move.got((2, "rest"))
        move.start(("core", 2, "one"))
        move.got((4, "rest"))
        move.start(("core", 4, "two"))
        move.got((2, "relay_edge"))
        move.z_start("up", 6)
        move.got((4, "relay_edge"))
        move.z_start("down", 6)
        move.got("core", ("core", 2, "one"), ("core", 2, "two"))
        move.got(("core", 4, "one"), ("core", 4, "two"))
        for d in (0, 2, 4):
            move.z_got(d)
        far_part(0, pairs - 2 * cap, 1)
        move.got((2, "relay_rest"))
        move.start(("core", 6, "one"))
        move.got((4, "relay_rest"))
        move.start(("core", 6, "two"))
        move.z_got(6, (0,))
        far_part(pairs - 2 * cap, pairs - cap, 2)
        move.got(("core", 6, "one"), ("core", 6, "two"))
        move.z_got(6, (1,))
        far_part(pairs - cap, pairs, 3)
        sent = move.kinds
    else:
        near_part(0, middle)
        near_part(middle, dates)
        plain_gather(n, me, strip, strips, grid, send, recv)
        far_part(0, pairs, 1)
        sent = 2 + 3 * (n - 1)

    across = lax.broadcasted_iota(I32, (pairs, width), 1)
    across = jnp.where(across < length, across, across - width).astype(F32) * 0.5
    cells = 1.0 / (width * width)
    held_columns = columns_v[...]
    lives = held_columns[:, 2 * chips:2 * chips + 1] > 0.5
    spread = spread_v[...]
    found = [None] * (2 * chips)
    for c in range(chips):
        held = sums[c]
        scale = jnp.sum(held, axis=1, keepdims=True) * cells + 1e-6
        low = jnp.sum(moments[c], axis=1, keepdims=True) * cells
        side = jnp.sum(held * across, axis=1, keepdims=True) * cells
        for x, value in enumerate((low, side)):
            k = x * chips + c
            found[k] = jnp.where(lives, held_columns[:, k:k + 1] + value / scale, 0.0)
            partial[k:k + 1] = jnp.sum(found[k] * spread, axis=0, keepdims=True)

    copies = []
    for j in range(1, n):
        where = {"date": lax.rem(me + j, n)}
        copies.append(remote(sent + j - 1, partial, held_sums.at[j - 1], where, send, recv))
        copies[-1].start()
    pick = picked[...]
    for x in range(2):
        for c in range(chips):
            offsets_out[x, c:c + 1] = jnp.sum(found[x * chips + c] * pick, axis=0, keepdims=True)
    total = partial[...]
    for j, copy in enumerate(copies):
        copy.wait_recv()
        total = total + held_sums[j]
    for x in range(2):
        for c in range(chips):
            k = x * chips + c
            value = jnp.sum(inverse[k] * total[k:k + 1], axis=1)[None]
            series_out[x, c:c + 1] = value
    if fast:
        move.left()
    for copy in copies:
        copy.wait_send()


def emit_kernel(offsets, series, offsets_out, series_out, done):
    copies = [
        pltpu.make_async_copy(a, b, done.at[k])
        for k, (a, b) in enumerate(((offsets, offsets_out), (series, series_out)))
    ]
    for copy in copies:
        copy.start()
    for copy in copies:
        copy.wait()


def body(n, strips, images, inverse, first, block, second, count, shifts, anchors):
    dates, length, cols = images.shape
    pairs, chips = first.shape[0], anchors.shape[0]
    vmem, anywhere = pl.BlockSpec(memory_space=pltpu.VMEM), pl.BlockSpec(memory_space=pl.ANY)
    tables = make_tables(length)
    fast = n == 8
    kinds = (33 if fast else 2 + 3 * (n - 1)) + n - 1
    width = 2 * length
    cap = 2 * pairs // n
    groups = length // SMAX + 2
    share = inverse.shape[2]
    block_shape = (groups, dates, SMAX, cols)
    late = block_shape if fast else (SMAX, cols)
    offsets, series = pl.pallas_call(
        functools.partial(pairs_kernel, n, strips, cap),
        name="pairs",
        out_shape=(
            pltpu.VMEM((2, chips, pairs), F32),
            pltpu.VMEM((2, chips, share), F32),
        ),
        in_specs=[anywhere] * 12,
        out_specs=(vmem, vmem),
        scratch_shapes=[
            pltpu.SMEM((1, pairs), I32),
            pltpu.SMEM((1, pairs), I32),
            pltpu.SMEM((1, pairs), I32),
            pltpu.SMEM((1,), I32),
            pltpu.SMEM((2, chips, pairs), I32),
            pltpu.SMEM((chips,), I32),
            pltpu.SMEM((1, pairs), I32),
            pltpu.VMEM((1, pairs), I32),
            pltpu.VMEM((1, pairs), I32),
            pltpu.VMEM((1, pairs), I32),
            pltpu.VMEM((2, chips, pairs), I32),
            pltpu.VMEM((2 * chips, share, n * dates), F32),
            *[pltpu.VMEM(table.shape, BF16) for table in tables],
            pltpu.VMEM((6 if fast else n, *block_shape), BF16),
            pltpu.VMEM(late, BF16),
            pltpu.VMEM(late, BF16),
            pltpu.VMEM((2 * chips, n * dates), F32),
            pltpu.VMEM((n - 1, 2 * chips, n * dates), F32),
            pltpu.SemaphoreType.DMA((groups + 14,)),
            pltpu.SemaphoreType.DMA((kinds,)),
            pltpu.SemaphoreType.DMA((kinds,)),
            pltpu.VMEM((pairs, length + 2 * SMAX, cols), F32),
            pltpu.VMEM((pairs * chips, length, cols), BF16),
            pltpu.VMEM((dates * chips, length, cols), BF16),
            pltpu.VMEM((dates * chips, length, 2 * width), BF16),
            pltpu.VMEM((chips, pairs, width), F32),
            pltpu.VMEM((chips, pairs, width), F32),
            pltpu.VMEM((pairs, pairs), F32),
            pltpu.VMEM((pairs, n * dates), F32),
            pltpu.VMEM((pairs, cols), F32),
            pltpu.VMEM((1, pairs), I32),
        ],
        compiler_params=pltpu.CompilerParams(collective_id=0, has_side_effects=True),
    )(
        first.reshape(1, pairs), block.reshape(1, pairs), second.reshape(1, pairs), count,
        jnp.transpose(shifts, (1, 2, 0)), anchors,
        images.reshape(dates, length // SMAX, SMAX, cols),
        inverse.reshape(2 * chips, share, n * dates), *tables,
    )
    offsets, series = pl.pallas_call(
        emit_kernel,
        name="emit",
        out_shape=(
            jax.ShapeDtypeStruct(offsets.shape, F32),
            jax.ShapeDtypeStruct(series.shape, F32),
        ),
        in_specs=[vmem] * 2,
        out_specs=(anywhere, anywhere),
        scratch_shapes=[pltpu.SemaphoreType.DMA((2,))],
    )(
        pltpu.with_memory_space_constraint(offsets, pltpu.VMEM),
        pltpu.with_memory_space_constraint(series, pltpu.VMEM),
    )
    return jnp.transpose(offsets, (2, 0, 1)), series


def solution(mesh):
    return jax.shard_map(
        functools.partial(body, mesh.shape["date"], mesh.shape["strip"]),
        mesh=mesh,
        in_specs=(
            P("date", "strip", None),
            P(None, "strip", "date", None),
            P("date"),
            P("date", None),
            P("date"),
            P("date"),
            P("date", None, "strip"),
            P("strip"),
        ),
        out_specs=(P("date", None, "strip"), P(None, "strip", "date")),
        check_vma=False,
    )
```

```python
import functools
import math

import jax
import jax.numpy as jnp
import numpy as np
from jax import lax
from jax.experimental import pallas as pl
from jax.experimental.pallas import tpu as pltpu
from jax.sharding import PartitionSpec as P

SMAX = 8
SPLIT = 8
PIECES = 1
MESH = pl.DeviceIdType.MESH
F32, BF16, I32 = jnp.float32, jnp.bfloat16, jnp.int32


def make_tables(length):
    counter = np.arange(length)
    radians = (counter[:, None] * counter[None, :] % length) * (2.0 * math.pi / length)
    cosine, sine = np.cos(radians), -np.sin(radians)
    over = 2 * length
    signed = np.where(counter < length // 2, counter, counter - length)
    places = np.arange(over)
    angles = (signed[:, None] * places[None, :] % over) * (2.0 * math.pi / over)
    vcos, vsin = np.cos(angles), np.sin(angles)
    forward = np.concatenate([cosine, sine], axis=1)
    empty = np.zeros_like(forward)
    forward = np.block([[forward, empty], [empty, forward]])
    rows = np.concatenate([cosine, sine], axis=1)
    one = np.concatenate([vcos, vsin], axis=1)
    two = np.concatenate([-vsin, vcos], axis=1)
    back = np.concatenate([one, one, two, -two], axis=0)
    final = np.concatenate([vcos.T, -vsin.T], axis=1)
    return [jnp.asarray(t.astype(np.float32)).astype(BF16) for t in (forward, rows, back, final)]


def remote(k, src, dst, where, send, recv):
    return pltpu.make_async_remote_copy(
        src_ref=src,
        dst_ref=dst,
        send_sem=send.at[k],
        recv_sem=recv.at[k],
        device_id=where,
        device_id_type=MESH,
    )


class Gather:
    def __init__(self, me, strip, strips, blocks, send, recv):
        self.blocks = blocks
        groups = blocks[0].shape[0]
        half = (groups - 2) // 2
        last = groups - 2
        self.has_up, self.has_down = strip > 0, strip < strips - 1
        up, down = lax.max(strip - 1, 0), lax.min(strip + 1, strips - 1)
        to = {j: jnp.bitwise_xor(me, j) for j in (1, 2, 4)}
        self.to, self.up, self.down = to, up, down
        self.copies = {}
        self.kinds = 0

        def add(name, d, at, many, where, target, dst_at=None):
            dst_at = at if dst_at is None else dst_at
            copy = remote(
                self.kinds,
                blocks[d].at[pl.ds(at, many)],
                blocks[target].at[pl.ds(dst_at, many)],
                where,
                send,
                recv,
            )
            self.copies[name] = copy
            self.kinds += 1

        edges = {"one": 1, "two": last}
        rests = {"one": 2, "two": 1 + half}
        inner = half - 1
        core = {"date": to[1]}
        add(("core", 0), 0, 1, 2 * half, core, 1)
        for link, now, later, relayed in ((4, "one", "two", 2), (2, "two", "one", 4)):
            where = {"date": to[link]}
            add((link, "now_edge"), 0, edges[now], 1, where, link)
            add((link, "now_rest"), 0, rests[now], inner, where, link)
            add((link, "later_edge"), 0, edges[later], 1, where, link)
            add((link, "relay_edge"), relayed, edges[later], 1, where, 6)
            begin = min(edges[now], rests[now])
            add(("core", link, "now"), link, begin, half, core, link ^ 1)
            add(("core", link, "edge"), link, edges[later], 1, core, link ^ 1)
            add(("core", 6, link, "edge"), 6, edges[later], 1, core, 7)
            for k in range(PIECES):
                many = inner // PIECES
                at = rests[later] + k * many
                add((link, "later_rest", k), 0, at, many, where, link)
                add((link, "relay_rest", k), relayed, at, many, where, 6)
                add(("core", link, "rest", k), link, at, many, core, link ^ 1)
                add(("core", 6, link, "rest", k), 6, at, many, core, 7)
        self.inner = PIECES
        for d in (0, 2, 4, 6):
            for flip in (0, 1):
                spot = {"date": jnp.bitwise_xor(me, flip)} if flip else {}
                add(("up", d, flip), d, 1, 1, {"strip": up, **spot}, d ^ flip, groups - 1)
                add(("down", d, flip), d, last, 1, {"strip": down, **spot}, d ^ flip, 0)

    def named(self, names):
        for key, copy in self.copies.items():
            if key in names or key[:2] in names:
                yield copy

    def start(self, *names):
        for copy in self.named(names):
            copy.start()

    def got(self, *names):
        for copy in self.named(names):
            copy.wait_recv()

    def z_start(self, side, d):
        has = self.has_up if side == "up" else self.has_down

        @pl.when(has)
        def _():
            for flip in (0, 1):
                self.copies[(side, d, flip)].start()

    def z_got(self, d, flips=(0, 1)):
        @pl.when(self.has_down)
        def _():
            for flip in flips:
                self.copies[("up", d, flip)].wait_recv()

        @pl.when(self.has_up)
        def _():
            for flip in flips:
                self.copies[("down", d, flip)].wait_recv()

    def left(self):
        for name, copy in self.copies.items():
            if name[0] == "up":
                pl.when(self.has_up)(copy.wait_send)
            elif name[0] == "down":
                pl.when(self.has_down)(copy.wait_send)
            else:
                copy.wait_send()


def plain_gather(n, me, strip, strips, grid, send, recv):
    groups = grid.shape[1]
    has_up, has_down = strip > 0, strip < strips - 1
    up, down = lax.max(strip - 1, 0), lax.min(strip + 1, strips - 1)
    z_up = remote(0, grid.at[me, 1], grid.at[me, groups - 1], {"strip": up}, send, recv)
    z_down = remote(1, grid.at[me, groups - 2], grid.at[me, 0], {"strip": down}, send, recv)
    pl.when(has_up)(z_up.start)
    pl.when(has_down)(z_down.start)
    copies = []
    peers = [{"date": lax.rem(me + j, n)} for j in range(1, n)]
    main = pl.ds(1, groups - 2)
    for j, peer in enumerate(peers):
        part = grid.at[me, main]
        copies.append(remote(2 + j, part, part, peer, send, recv))
        copies[-1].start()
    pl.when(has_down)(z_up.wait_recv)
    pl.when(has_up)(z_down.wait_recv)
    pl.when(has_up)(z_up.wait_send)
    pl.when(has_down)(z_down.wait_send)
    for side, at in ((0, 0), (1, groups - 1)):
        for j, peer in enumerate(peers):
            part = grid.at[me, at]
            copies.append(remote(2 + (1 + side) * (n - 1) + j, part, part, peer, send, recv))
            copies[-1].start()
    for copy in copies:
        copy.wait()


def pairs_kernel(
    n, strips, cap,
    first_h, block_h, second_h, count_h, shifts_h, anchors_h,
    img, inverse_h, forward_h, rows_h, back_h, final_h,
    offsets_out, series_out,
    first_s, block_s, second_s, count_s, shifts_s, anchors_s, perm_s,
    first_v, block_v, second_v, shifts_v, inverse, forward, rows, back, final,
    grid, late, partial, held_sums,
    local, send, recv,
    wide, far, near, spec, far_spec, sums, moments, picked, spread_v, columns_v, perm_v,
):
    groups, dates, _, cols = grid.shape[1:]
    length = SMAX * (groups - 2)
    pairs, chips = first_s.shape[1], anchors_s.shape[0]
    fast = n == 8
    me, strip = lax.axis_index("date"), lax.axis_index("strip")
    has_up, has_down = strip > 0, strip < strips - 1
    up, down = lax.max(strip - 1, 0), lax.min(strip + 1, strips - 1)

    barrier = pltpu.get_barrier_semaphore()
    if fast:
        greeted = [{"date": jnp.bitwise_xor(me, j)} for j in (1, 2, 4)]
        side_spots = [{}, {"date": jnp.bitwise_xor(me, 1)}]
    else:
        greeted = [{"date": lax.rem(me + j, n)} for j in range(1, n)]
        side_spots = [{}]
    for where in greeted:
        pl.semaphore_signal(barrier, inc=1, device_id=where, device_id_type=MESH)
    for other, has in ((up, has_up), (down, has_down)):
        @pl.when(has)
        def _():
            for spot in side_spots:
                pl.semaphore_signal(
                    barrier, inc=1, device_id={"strip": other, **spot}, device_id_type=MESH
                )

    count = iter(range(local.shape[0]))

    def load(src, dst):
        copy = pltpu.make_async_copy(src, dst, local.at[next(count)])
        copy.start()
        return copy

    own = 0 if fast else me
    spots = [0, groups - 3, *range(1, groups - 3)]
    mine = [load(img.at[:, g], grid.at[own, 1 + g]) for g in spots]
    small = [
        load(a, b)
        for a, b in (
            (first_h, first_s), (block_h, block_s), (second_h, second_s), (count_h, count_s),
            (shifts_h, shifts_s), (anchors_h, anchors_s),
            (first_h, first_v), (block_h, block_v), (second_h, second_v), (shifts_h, shifts_v),
        )
    ]
    large = [
        load(a, b)
        for a, b in (
            (forward_h, forward), (rows_h, rows), (back_h, back), (final_h, final),
            (inverse_h, inverse),
        )
    ]
    sides = len(side_spots) * (has_up.astype(I32) + has_down.astype(I32))
    pl.semaphore_wait(barrier, len(greeted) + sides)
    for copy in mine[:2]:
        copy.wait()
    if fast:
        blocks = [grid.at[d] for d in range(6)] + [late.at[d] for d in range(2)]
        move = Gather(me, strip, strips, blocks, send, recv)
        move.start((4, "now_edge"), (2, "now_edge"))
        move.start((4, "later_edge"), (2, "later_edge"))
        move.z_start("up", 0)
        move.z_start("down", 0)
    for copy in mine[2:]:
        copy.wait()
    if fast:
        move.start((4, "now_rest"), (2, "now_rest"), ("core", 0))
    for copy in small + large:
        copy.wait()

    line = lax.broadcasted_iota(I32, (pairs, pairs), 0)
    place = lax.broadcasted_iota(I32, (pairs, pairs), 1)
    if fast:
        distance = jnp.bitwise_xor(block_v[...], me)
        key = jnp.broadcast_to(jnp.maximum(distance - 5, 0), (pairs, pairs))
        key_line = jnp.sum(jnp.where(line == place, key, 0), axis=1, keepdims=True)
        ahead = (key < key_line) | ((key == key_line) & (place < line))
        rank_line = jnp.sum(ahead.astype(I32), axis=1, keepdims=True)
        behind = (key_line < key) | ((key_line == key) & (line < place))
        rank = jnp.sum(behind.astype(I32), axis=0, keepdims=True)
        perm_v[...] = jnp.sum(jnp.where(rank_line == place, line, 0), axis=0, keepdims=True)
        ordered = load(perm_v, perm_s)
        pick = (jnp.broadcast_to(rank, (pairs, pairs)) == line).astype(F32)
    else:
        pick = (line == place).astype(F32)
    picked[...] = pick

    def chosen(row):
        return jnp.sum(pick * row, axis=1, keepdims=True)

    spot = lax.broadcasted_iota(I32, (pairs, partial.shape[1]), 1).astype(F32)
    to_date = chosen((block_v[...] * dates + second_v[...]).astype(F32))
    from_date = chosen((me * dates + first_v[...]).astype(F32))
    spread_v[...] = (spot == to_date).astype(F32) - (spot == from_date).astype(F32)
    live = (lax.broadcasted_iota(I32, (1, pairs), 1) < count_s[0]).astype(F32)
    at = lax.broadcasted_iota(I32, columns_v.shape, 1)
    held_columns = jnp.where(at == 2 * chips, chosen(live), 0.0)
    for x in range(2):
        for c in range(chips):
            column = chosen(shifts_v[x, c:c + 1].astype(F32))
            held_columns = jnp.where(at == x * chips + c, column, held_columns)
    columns_v[...] = held_columns

    lane = lax.broadcasted_iota(I32, (1, cols), 1)
    left_half = lane < length

    def paired(one, start_one, two, start_two):
        one = pltpu.roll(one, lax.rem(2 * cols - start_one, cols), 1)
        two = pltpu.roll(two, lax.rem(2 * cols + length - start_two, cols), 1)
        column = jnp.where(left_half, start_one + lane, start_two - length + lane)
        inside = jnp.where((column >= 0) & (column < cols), 1.0, 0.0)
        both = jnp.where(jnp.broadcast_to(left_half, one.shape), one, two)
        return (both * inside).astype(BF16)

    width = 2 * length
    lanes2 = lax.broadcasted_iota(I32, (1, 2 * width), 1)
    base = jnp.where((lanes2 == 0) | (lanes2 == width), 1.0 / length, 0.0)
    turn_sign = jnp.where(left_half, -1.0, 1.0).astype(BF16)

    def split(many, size):
        step = max(1, many // SPLIT) * size
        return [(at, step) for at in range(0, many * size, step)]

    def spectra(ref, at, many):
        windows = ref[pl.ds(at, many)].reshape(many * length, cols)
        sections = []
        for start, size in split(many, length):
            found = jnp.dot(windows[start:start + size], forward[...], preferred_element_type=F32)
            sections += [found[k:k + length] for k in range(0, size, length)]
        stacked = []
        for part in sections:
            part = part - jnp.sum(part, axis=0, keepdims=True) * base
            for c in range(2):
                top = part[:, c * width:(c + 1) * width]
                low = pltpu.roll(top, length, 1).astype(BF16) * turn_sign
                stacked.append(jnp.concatenate([top.astype(BF16), low], axis=0))
        found = []
        for start, size in split(many, 2):
            both = jnp.concatenate(stacked[start:start + size], axis=1)
            both = jnp.dot(rows[...], both, preferred_element_type=F32)
            found += [both[:, k * width:(k + 1) * width] for k in range(size)]
        return found

    def near_part(low, high):
        for d in range(low, high):
            value = grid[own, pl.ds(1, groups - 2), d].astype(F32).reshape(length, cols)
            near[d] = paired(value, anchors_s[0], value, anchors_s[1])
        found = spectra(near, low, high - low)
        for w in range((high - low) * chips):
            both = jnp.concatenate([found[w], pltpu.roll(found[w], length, 1)], axis=1)
            spec[low * chips + w] = both.astype(BF16)

    def far_cut(i, stage):
        p = perm_s[0, i] if fast else i
        block, day = block_s[0, p], second_s[0, p]
        if fast:
            distance = jnp.bitwise_xor(block, me)
            value = grid[jnp.where(distance < 6, distance, 0), :, day].astype(F32)
            if stage > 1:
                other = late[jnp.where(distance == 7, 1, 0), :, day].astype(F32)
                value = jnp.where(distance < 6, value, other)
        else:
            value = grid[block, :, day].astype(F32)
        wide[i, pl.ds(0, SMAX)] = jnp.where(has_up, value[0], 0.0)
        wide[i, pl.ds(SMAX, length)] = value[1:groups - 1].reshape(length, cols)
        wide[i, pl.ds(SMAX + length, SMAX)] = jnp.where(has_down, value[groups - 1], 0.0)
        windows = []
        for c in range(2):
            windows.append(wide[i, pl.ds(SMAX + shifts_s[0, c, p], length)])
            windows.append(anchors_s[c] + shifts_s[1, c, p])
        far[i] = paired(*windows)

    tiles = width // SMAX
    row_in = lax.broadcasted_iota(I32, (SMAX, width), 0).astype(F32) * 0.5
    row_in = row_in - (tiles // 2 + 1) * (SMAX // 2)

    def far_spectra(low, high, stage):
        for i in range(low, high):
            far_cut(i, stage)
        found = spectra(far, low, high - low)
        for w, value in enumerate(found):
            far_spec[low * chips + w] = value.astype(BF16)

    def far_centres(low, high):
        many = (high - low) * chips
        crossed = []
        for i in range(low, high):
            day = first_s[0, perm_s[0, i] if fast else i]
            for c in range(chips):
                value = far_spec[i * chips + c]
                crossed.append(spec[day * chips + c] * jnp.concatenate([value, value], axis=1))
        stacked = []
        for start, size in split(many, 1):
            along = jnp.concatenate(crossed[start:start + size], axis=0)
            along = jnp.dot(along, back[...], preferred_element_type=F32).astype(BF16)
            for w in range(size):
                part = along[w * length:(w + 1) * length]
                stacked.append(jnp.concatenate([part[:, :width], part[:, width:]], axis=0))
        surfaces = []
        for start, size in split(many, 1):
            both = jnp.concatenate(stacked[start:start + size], axis=1)
            both = jnp.dot(final[...], both, preferred_element_type=F32)
            surfaces += [both[:, k * width:(k + 1) * width] for k in range(size)]
        for b in range(high - low):
            for c in range(chips):
                w = b * chips + c
                value = surfaces[w]
                run, ramp = None, None
                for t in (*range(tiles // 2 - 1, -1, -1), *range(tiles - 1, tiles // 2 - 1, -1)):
                    energy = value[t * SMAX:(t + 1) * SMAX]
                    energy = energy * energy
                    run = energy if run is None else run + energy
                    ramp = run if ramp is None else ramp + run
                at = (c, pl.ds(low + b, 1))
                sums[at] = jnp.sum(run, axis=0, keepdims=True)
                weighted = ramp * (SMAX // 2) + run * row_in
                moments[at] = jnp.sum(weighted, axis=0, keepdims=True)

    middle = dates // 2
    if fast:
        near_part(0, middle)
        for link, side in ((2, "down"), (4, "up")):
            move.got((link, "now_edge"))
            move.start((6 - link, "relay_edge"))
            move.z_start(side, link)
        move.start((4, "later_rest"), (2, "later_rest"))
        for link, side in ((2, "up"), (4, "down")):
            move.got((link, "later_edge"))
            move.z_start(side, link)
            move.start(("core", link, "edge"))
        near_part(middle, dates)
        for link in (2, 4):
            move.got((link, "now_rest"))
            move.start((6 - link, "relay_rest"), ("core", link, "now"))
        ordered.wait()
        for link, side in ((2, "up"), (4, "down")):
            move.got((link, "relay_edge"))
            move.z_start(side, 6)
            move.start(("core", 6, link, "edge"))
        for k in range(move.inner):
            for link in (2, 4):
                move.got((link, "later_rest", k))
                move.start(("core", link, "rest", k))
        move.got(("core", 0), ("core", 2), ("core", 4))
        for d in (0, 2, 4):
            move.z_got(d)

        def hand_on(*pieces):
            for k in pieces:
                for link in (2, 4):
                    move.got((link, "relay_rest", k))
                    move.start(("core", 6, link, "rest", k))

        early = pairs - 2 * cap
        far_spectra(0, early, 1)
        hand_on(*range(move.inner))
        far_centres(0, early)
        move.got(("core", 6))
        move.z_got(6)
        far_spectra(early, pairs, 2)
        far_centres(early, pairs)
        sent = move.kinds
    else:
        near_part(0, middle)
        near_part(middle, dates)
        plain_gather(n, me, strip, strips, grid, send, recv)
        far_spectra(0, pairs, 1)
        far_centres(0, pairs)
        sent = 2 + 3 * (n - 1)

    across = lax.broadcasted_iota(I32, (pairs, width), 1)
    across = jnp.where(across < length, across, across - width).astype(F32) * 0.5
    cells = 1.0 / (width * width)
    held_columns = columns_v[...]
    lives = held_columns[:, 2 * chips:2 * chips + 1] > 0.5
    spread = spread_v[...]
    found = [None] * (2 * chips)
    for c in range(chips):
        held = sums[c]
        scale = jnp.sum(held, axis=1, keepdims=True) * cells + 1e-6
        low = jnp.sum(moments[c], axis=1, keepdims=True) * cells
        side = jnp.sum(held * across, axis=1, keepdims=True) * cells
        for x, value in enumerate((low, side)):
            k = x * chips + c
            found[k] = jnp.where(lives, held_columns[:, k:k + 1] + value / scale, 0.0)
            partial[k:k + 1] = jnp.sum(found[k] * spread, axis=0, keepdims=True)

    copies = []
    for j in range(1, n):
        where = {"date": lax.rem(me + j, n)}
        copies.append(remote(sent + j - 1, partial, held_sums.at[j - 1], where, send, recv))
        copies[-1].start()
    pick = picked[...]
    for x in range(2):
        for c in range(chips):
            offsets_out[x, c:c + 1] = jnp.sum(found[x * chips + c] * pick, axis=0, keepdims=True)
    total = partial[...]
    for j, copy in enumerate(copies):
        copy.wait_recv()
        total = total + held_sums[j]
    for x in range(2):
        for c in range(chips):
            k = x * chips + c
            value = jnp.sum(inverse[k] * total[k:k + 1], axis=1)[None]
            series_out[x, c:c + 1] = value
    if fast:
        move.left()
    for copy in copies:
        copy.wait_send()


def emit_kernel(offsets, series, offsets_out, series_out, done):
    copies = [
        pltpu.make_async_copy(a, b, done.at[k])
        for k, (a, b) in enumerate(((offsets, offsets_out), (series, series_out)))
    ]
    for copy in copies:
        copy.start()
    for copy in copies:
        copy.wait()


def body(n, strips, images, inverse, first, block, second, count, shifts, anchors):
    dates, length, cols = images.shape
    pairs, chips = first.shape[0], anchors.shape[0]
    vmem, anywhere = pl.BlockSpec(memory_space=pltpu.VMEM), pl.BlockSpec(memory_space=pl.ANY)
    tables = make_tables(length)
    fast = n == 8
    half = length // SMAX // 2
    kinds = (17 + 14 + 8 * PIECES if fast else 2 + 3 * (n - 1)) + n - 1
    width = 2 * length
    cap = 2 * pairs // n
    groups = length // SMAX + 2
    share = inverse.shape[2]
    block_shape = (groups, dates, SMAX, cols)
    late = (2, *block_shape) if fast else (SMAX, cols)
    offsets, series = pl.pallas_call(
        functools.partial(pairs_kernel, n, strips, cap),
        name="pairs",
        out_shape=(
            pltpu.VMEM((2, chips, pairs), F32),
            pltpu.VMEM((2, chips, share), F32),
        ),
        in_specs=[anywhere] * 12,
        out_specs=(vmem, vmem),
        scratch_shapes=[
            pltpu.SMEM((1, pairs), I32),
            pltpu.SMEM((1, pairs), I32),
            pltpu.SMEM((1, pairs), I32),
            pltpu.SMEM((1,), I32),
            pltpu.SMEM((2, chips, pairs), I32),
            pltpu.SMEM((chips,), I32),
            pltpu.SMEM((1, pairs), I32),
            pltpu.VMEM((1, pairs), I32),
            pltpu.VMEM((1, pairs), I32),
            pltpu.VMEM((1, pairs), I32),
            pltpu.VMEM((2, chips, pairs), I32),
            pltpu.VMEM((2 * chips, share, n * dates), F32),
            *[pltpu.VMEM(table.shape, BF16) for table in tables],
            pltpu.VMEM((6 if fast else n, *block_shape), BF16),
            pltpu.VMEM(late, BF16),
            pltpu.VMEM((2 * chips, n * dates), F32),
            pltpu.VMEM((n - 1, 2 * chips, n * dates), F32),
            pltpu.SemaphoreType.DMA((groups + 14,)),
            pltpu.SemaphoreType.DMA((kinds,)),
            pltpu.SemaphoreType.DMA((kinds,)),
            pltpu.VMEM((pairs, length + 2 * SMAX, cols), F32),
            pltpu.VMEM((pairs, length, cols), BF16),
            pltpu.VMEM((dates, length, cols), BF16),
            pltpu.VMEM((dates * chips, length, 2 * width), BF16),
            pltpu.VMEM((pairs * chips, length, width), BF16),
            pltpu.VMEM((chips, pairs, width), F32),
            pltpu.VMEM((chips, pairs, width), F32),
            pltpu.VMEM((pairs, pairs), F32),
            pltpu.VMEM((pairs, n * dates), F32),
            pltpu.VMEM((pairs, cols), F32),
            pltpu.VMEM((1, pairs), I32),
        ],
        compiler_params=pltpu.CompilerParams(collective_id=0, has_side_effects=True),
    )(
        first.reshape(1, pairs), block.reshape(1, pairs), second.reshape(1, pairs), count,
        jnp.transpose(shifts, (1, 2, 0)), anchors,
        images.reshape(dates, length // SMAX, SMAX, cols),
        inverse.reshape(2 * chips, share, n * dates), *tables,
    )
    offsets, series = pl.pallas_call(
        emit_kernel,
        name="emit",
        out_shape=(
            jax.ShapeDtypeStruct(offsets.shape, F32),
            jax.ShapeDtypeStruct(series.shape, F32),
        ),
        in_specs=[vmem] * 2,
        out_specs=(anywhere, anywhere),
        scratch_shapes=[pltpu.SemaphoreType.DMA((2,))],
    )(
        pltpu.with_memory_space_constraint(offsets, pltpu.VMEM),
        pltpu.with_memory_space_constraint(series, pltpu.VMEM),
    )
    return jnp.transpose(offsets, (2, 0, 1)), series


def solution(mesh):
    return jax.shard_map(
        functools.partial(body, mesh.shape["date"], mesh.shape["strip"]),
        mesh=mesh,
        in_specs=(
            P("date", "strip", None),
            P(None, "strip", "date", None),
            P("date"),
            P("date", None),
            P("date"),
            P("date"),
            P("date", None, "strip"),
            P("strip"),
        ),
        out_specs=(P("date", None, "strip"), P(None, "strip", "date")),
        check_vma=False,
    )
```

```python
import functools
import math

import jax
import jax.numpy as jnp
import numpy as np
from jax import lax
from jax.experimental import pallas as pl
from jax.experimental.pallas import tpu as pltpu
from jax.sharding import PartitionSpec as P

SMAX = 8
SPLIT = 8
PIECES = 1
MESH = pl.DeviceIdType.MESH
F32, BF16, I32 = jnp.float32, jnp.bfloat16, jnp.int32


def make_tables(length):
    counter = np.arange(length)
    radians = (counter[:, None] * counter[None, :] % length) * (2.0 * math.pi / length)
    cosine, sine = np.cos(radians), -np.sin(radians)
    over = 2 * length
    signed = np.where(counter < length // 2, counter, counter - length)
    places = np.arange(over)
    angles = (signed[:, None] * places[None, :] % over) * (2.0 * math.pi / over)
    vcos, vsin = np.cos(angles), np.sin(angles)
    forward = np.concatenate([cosine, sine], axis=1)
    empty = np.zeros_like(forward)
    forward = np.block([[forward, empty], [empty, forward]])
    half = length // 2
    kept = -(-(half + 1) // 16) * 16
    rows = np.zeros((kept, over))
    rows[:half + 1] = np.concatenate([cosine, sine], axis=1)[:half + 1]
    vsin[half] = 0.0
    one = np.concatenate([vcos, vsin], axis=1)
    two = np.concatenate([-vsin, vcos], axis=1)
    back = np.concatenate([one, one, two, -two], axis=0)
    lean = ((places + length) % over - length) * 0.5
    waves = counter[:half + 1, None] * places[None, :] * (2.0 * math.pi / over)
    even = np.where((counter[:half + 1] == 0) | (counter[:half + 1] == half), 1.0, 2.0)
    odd = np.where(counter[:half + 1] == half, 1.0, -2.0)
    final = np.zeros((kept, kept))
    final[:half + 1, :half + 1] = 2.0 * (even[:, None] * np.cos(waves) * lean) @ (
        odd[:, None] * np.sin(waves)
    ).T
    return [jnp.asarray(t.astype(np.float32)).astype(BF16) for t in (forward, rows, back, final)]


def remote(k, src, dst, where, send, recv):
    return pltpu.make_async_remote_copy(
        src_ref=src,
        dst_ref=dst,
        send_sem=send.at[k],
        recv_sem=recv.at[k],
        device_id=where,
        device_id_type=MESH,
    )


class Gather:
    def __init__(self, me, strip, strips, blocks, send, recv):
        self.blocks = blocks
        groups = blocks[0].shape[0]
        half = (groups - 2) // 2
        last = groups - 2
        self.has_up, self.has_down = strip > 0, strip < strips - 1
        up, down = lax.max(strip - 1, 0), lax.min(strip + 1, strips - 1)
        to = {j: jnp.bitwise_xor(me, j) for j in (1, 2, 4)}
        self.to, self.up, self.down = to, up, down
        self.copies = {}
        self.kinds = 0

        def add(name, d, at, many, where, target, dst_at=None):
            dst_at = at if dst_at is None else dst_at
            copy = remote(
                self.kinds,
                blocks[d].at[pl.ds(at, many)],
                blocks[target].at[pl.ds(dst_at, many)],
                where,
                send,
                recv,
            )
            self.copies[name] = copy
            self.kinds += 1

        edges = {"one": 1, "two": last}
        rests = {"one": 2, "two": 1 + half}
        inner = half - 1
        core = {"date": to[1]}
        add(("core", 0), 0, 1, 2 * half, core, 1)
        for link, now, later, relayed in ((4, "one", "two", 2), (2, "two", "one", 4)):
            where = {"date": to[link]}
            add((link, "now_edge"), 0, edges[now], 1, where, link)
            add((link, "now_rest"), 0, rests[now], inner, where, link)
            add((link, "later_edge"), 0, edges[later], 1, where, link)
            add((link, "relay_edge"), relayed, edges[later], 1, where, 6)
            begin = min(edges[now], rests[now])
            add(("core", link, "now"), link, begin, half, core, link ^ 1)
            add(("core", link, "edge"), link, edges[later], 1, core, link ^ 1)
            add(("core", 6, link, "edge"), 6, edges[later], 1, core, 7)
            for k in range(PIECES):
                many = inner // PIECES
                at = rests[later] + k * many
                add((link, "later_rest", k), 0, at, many, where, link)
                add((link, "relay_rest", k), relayed, at, many, where, 6)
                add(("core", link, "rest", k), link, at, many, core, link ^ 1)
                add(("core", 6, link, "rest", k), 6, at, many, core, 7)
        self.inner = PIECES
        for d in (0, 2, 4, 6):
            for flip in (0, 1):
                spot = {"date": jnp.bitwise_xor(me, flip)} if flip else {}
                add(("up", d, flip), d, 1, 1, {"strip": up, **spot}, d ^ flip, groups - 1)
                add(("down", d, flip), d, last, 1, {"strip": down, **spot}, d ^ flip, 0)

    def named(self, names):
        for key, copy in self.copies.items():
            if key in names or key[:2] in names:
                yield copy

    def start(self, *names):
        for copy in self.named(names):
            copy.start()

    def got(self, *names):
        for copy in self.named(names):
            copy.wait_recv()

    def z_start(self, side, d):
        has = self.has_up if side == "up" else self.has_down

        @pl.when(has)
        def _():
            for flip in (0, 1):
                self.copies[(side, d, flip)].start()

    def z_got(self, d, flips=(0, 1)):
        @pl.when(self.has_down)
        def _():
            for flip in flips:
                self.copies[("up", d, flip)].wait_recv()

        @pl.when(self.has_up)
        def _():
            for flip in flips:
                self.copies[("down", d, flip)].wait_recv()

    def left(self):
        for name, copy in self.copies.items():
            if name[0] == "up":
                pl.when(self.has_up)(copy.wait_send)
            elif name[0] == "down":
                pl.when(self.has_down)(copy.wait_send)
            else:
                copy.wait_send()


def plain_gather(n, me, strip, strips, grid, send, recv):
    groups = grid.shape[1]
    has_up, has_down = strip > 0, strip < strips - 1
    up, down = lax.max(strip - 1, 0), lax.min(strip + 1, strips - 1)
    z_up = remote(0, grid.at[me, 1], grid.at[me, groups - 1], {"strip": up}, send, recv)
    z_down = remote(1, grid.at[me, groups - 2], grid.at[me, 0], {"strip": down}, send, recv)
    pl.when(has_up)(z_up.start)
    pl.when(has_down)(z_down.start)
    copies = []
    peers = [{"date": lax.rem(me + j, n)} for j in range(1, n)]
    main = pl.ds(1, groups - 2)
    for j, peer in enumerate(peers):
        part = grid.at[me, main]
        copies.append(remote(2 + j, part, part, peer, send, recv))
        copies[-1].start()
    pl.when(has_down)(z_up.wait_recv)
    pl.when(has_up)(z_down.wait_recv)
    pl.when(has_up)(z_up.wait_send)
    pl.when(has_down)(z_down.wait_send)
    for side, at in ((0, 0), (1, groups - 1)):
        for j, peer in enumerate(peers):
            part = grid.at[me, at]
            copies.append(remote(2 + (1 + side) * (n - 1) + j, part, part, peer, send, recv))
            copies[-1].start()
    for copy in copies:
        copy.wait()


def pairs_kernel(
    n, strips, cap,
    first_h, block_h, second_h, count_h, shifts_h, anchors_h,
    img, inverse_h, forward_h, rows_h, back_h, final_h,
    offsets_out, series_out,
    first_s, block_s, second_s, count_s, shifts_s, anchors_s, perm_s,
    first_v, block_v, second_v, shifts_v, inverse, forward, rows, back, final,
    grid, late, partial, held_sums,
    local, send, recv,
    wide, far, near, spec, far_spec, sums, moments, picked, spread_v, columns_v, perm_v,
):
    groups, dates, _, cols = grid.shape[1:]
    length = SMAX * (groups - 2)
    pairs, chips = first_s.shape[1], anchors_s.shape[0]
    fast = n == 8
    me, strip = lax.axis_index("date"), lax.axis_index("strip")
    has_up, has_down = strip > 0, strip < strips - 1
    up, down = lax.max(strip - 1, 0), lax.min(strip + 1, strips - 1)

    barrier = pltpu.get_barrier_semaphore()
    if fast:
        greeted = [{"date": jnp.bitwise_xor(me, j)} for j in (1, 2, 4)]
        side_spots = [{}, {"date": jnp.bitwise_xor(me, 1)}]
    else:
        greeted = [{"date": lax.rem(me + j, n)} for j in range(1, n)]
        side_spots = [{}]
    for where in greeted:
        pl.semaphore_signal(barrier, inc=1, device_id=where, device_id_type=MESH)
    for other, has in ((up, has_up), (down, has_down)):
        @pl.when(has)
        def _():
            for spot in side_spots:
                pl.semaphore_signal(
                    barrier, inc=1, device_id={"strip": other, **spot}, device_id_type=MESH
                )

    count = iter(range(local.shape[0]))

    def load(src, dst):
        copy = pltpu.make_async_copy(src, dst, local.at[next(count)])
        copy.start()
        return copy

    own = 0 if fast else me
    spots = [0, groups - 3, *range(1, groups - 3)]
    mine = [load(img.at[:, g], grid.at[own, 1 + g]) for g in spots]
    small = [
        load(a, b)
        for a, b in (
            (first_h, first_s), (block_h, block_s), (second_h, second_s), (count_h, count_s),
            (shifts_h, shifts_s), (anchors_h, anchors_s),
            (first_h, first_v), (block_h, block_v), (second_h, second_v), (shifts_h, shifts_v),
        )
    ]
    large = [
        load(a, b)
        for a, b in (
            (forward_h, forward), (rows_h, rows), (back_h, back), (final_h, final),
            (inverse_h, inverse),
        )
    ]
    sides = len(side_spots) * (has_up.astype(I32) + has_down.astype(I32))
    pl.semaphore_wait(barrier, len(greeted) + sides)
    for copy in mine[:2]:
        copy.wait()
    if fast:
        blocks = [grid.at[d] for d in range(6)] + [late.at[d] for d in range(2)]
        move = Gather(me, strip, strips, blocks, send, recv)
        move.start((4, "now_edge"), (2, "now_edge"))
        move.start((4, "later_edge"), (2, "later_edge"))
        move.z_start("up", 0)
        move.z_start("down", 0)
    for copy in mine[2:]:
        copy.wait()
    if fast:
        move.start((4, "now_rest"), (2, "now_rest"), ("core", 0))
    for copy in small + large:
        copy.wait()

    line = lax.broadcasted_iota(I32, (pairs, pairs), 0)
    place = lax.broadcasted_iota(I32, (pairs, pairs), 1)
    if fast:
        distance = jnp.bitwise_xor(block_v[...], me)
        key = jnp.broadcast_to(jnp.maximum(distance - 5, 0), (pairs, pairs))
        key_line = jnp.sum(jnp.where(line == place, key, 0), axis=1, keepdims=True)
        ahead = (key < key_line) | ((key == key_line) & (place < line))
        rank_line = jnp.sum(ahead.astype(I32), axis=1, keepdims=True)
        behind = (key_line < key) | ((key_line == key) & (line < place))
        rank = jnp.sum(behind.astype(I32), axis=0, keepdims=True)
        perm_v[...] = jnp.sum(jnp.where(rank_line == place, line, 0), axis=0, keepdims=True)
        ordered = load(perm_v, perm_s)
        pick = (jnp.broadcast_to(rank, (pairs, pairs)) == line).astype(F32)
    else:
        pick = (line == place).astype(F32)
    picked[...] = pick

    def chosen(row):
        return jnp.sum(pick * row, axis=1, keepdims=True)

    spot = lax.broadcasted_iota(I32, (pairs, partial.shape[1]), 1).astype(F32)
    to_date = chosen((block_v[...] * dates + second_v[...]).astype(F32))
    from_date = chosen((me * dates + first_v[...]).astype(F32))
    spread_v[...] = (spot == to_date).astype(F32) - (spot == from_date).astype(F32)
    live = (lax.broadcasted_iota(I32, (1, pairs), 1) < count_s[0]).astype(F32)
    at = lax.broadcasted_iota(I32, columns_v.shape, 1)
    held_columns = jnp.where(at == 2 * chips, chosen(live), 0.0)
    for x in range(2):
        for c in range(chips):
            column = chosen(shifts_v[x, c:c + 1].astype(F32))
            held_columns = jnp.where(at == x * chips + c, column, held_columns)
    columns_v[...] = held_columns

    lane = lax.broadcasted_iota(I32, (1, cols), 1)
    left_half = lane < length

    def paired(one, start_one, two, start_two):
        one = pltpu.roll(one.astype(BF16), lax.rem(2 * cols - start_one, cols), 1)
        two = pltpu.roll(two.astype(BF16), lax.rem(2 * cols + length - start_two, cols), 1)
        column = jnp.where(left_half, start_one + lane, start_two - length + lane)
        inside = (column >= 0) & (column < cols)
        keep_one = jnp.where(left_half & inside, 1.0, 0.0).astype(BF16)
        keep_two = jnp.where(left_half, 0.0, jnp.where(inside, 1.0, 0.0)).astype(BF16)
        return one * keep_one + two * keep_two

    width = 2 * length
    lanes2 = lax.broadcasted_iota(I32, (1, 2 * width), 1)
    base = jnp.where((lanes2 == 0) | (lanes2 == width), 1.0 / length, 0.0)
    turn_sign = jnp.where(left_half, -1.0, 1.0).astype(BF16)

    def split(many, size):
        step = max(1, many // SPLIT) * size
        return [(at, step) for at in range(0, many * size, step)]

    def spectra(ref, at, many):
        windows = ref[pl.ds(at, many)].reshape(many * length, cols)
        sections = []
        for start, size in split(many, length):
            found = jnp.dot(windows[start:start + size], forward[...], preferred_element_type=F32)
            sections += [found[k:k + length] for k in range(0, size, length)]
        stacked = []
        for part in sections:
            part = part - jnp.sum(part, axis=0, keepdims=True) * base
            for c in range(2):
                top = part[:, c * width:(c + 1) * width]
                top = top.astype(BF16)
                low = pltpu.roll(top, length, 1) * turn_sign
                stacked.append(jnp.concatenate([top, low], axis=0))
        found = []
        for start, size in split(many, 2):
            both = jnp.concatenate(stacked[start:start + size], axis=1)
            both = jnp.dot(rows[...], both, preferred_element_type=F32)
            found += [both[:, k * width:(k + 1) * width] for k in range(size)]
        return found

    def near_part(low, high):
        for d in range(low, high):
            value = grid[own, pl.ds(1, groups - 2), d].astype(F32).reshape(length, cols)
            near[d] = paired(value, anchors_s[0], value, anchors_s[1])
        found = spectra(near, low, high - low)
        for w in range((high - low) * chips):
            both = jnp.concatenate([found[w], pltpu.roll(found[w], length, 1)], axis=1)
            spec[low * chips + w] = both.astype(BF16)

    def far_cut(i, stage):
        p = perm_s[0, i] if fast else i
        block, day = block_s[0, p], second_s[0, p]
        if fast:
            distance = jnp.bitwise_xor(block, me)
            value = grid[jnp.where(distance < 6, distance, 0), :, day].astype(F32)
            if stage > 1:
                other = late[jnp.where(distance == 7, 1, 0), :, day].astype(F32)
                value = jnp.where(distance < 6, value, other)
        else:
            value = grid[block, :, day].astype(F32)
        wide[i, pl.ds(0, SMAX)] = jnp.where(has_up, value[0], 0.0)
        wide[i, pl.ds(SMAX, length)] = value[1:groups - 1].reshape(length, cols)
        wide[i, pl.ds(SMAX + length, SMAX)] = jnp.where(has_down, value[groups - 1], 0.0)
        windows = []
        for c in range(2):
            windows.append(wide[i, pl.ds(SMAX + shifts_s[0, c, p], length)])
            windows.append(anchors_s[c] + shifts_s[1, c, p])
        far[i] = paired(*windows)

    kept, nyquist = rows.shape[0], length // 2
    tiles = nyquist // SMAX
    row_in = lax.broadcasted_iota(I32, (SMAX, width), 0)
    lane_in = lax.broadcasted_iota(I32, (SMAX, width), 1)
    top = row_in == 0
    real_weight, imag_weight = jnp.where(top, 0.5, 1.0), jnp.where(top, 0.0, 1.0)
    edge_weight, flip = jnp.where(top, 1.0, 2.0), jnp.where(lax.rem(row_in, 2) == 0, 1.0, -1.0)
    corner = jnp.where(top & (lax.rem(lane_in, length) == nyquist), 1.0, 0.0)
    quarter = lax.rem(lane_in, 4)
    corner_wave = jnp.where(quarter == 1, -1.0, jnp.where(quarter == 3, 1.0, 0.0))

    def tile(value, t):
        return value[t * SMAX:(t + 1) * SMAX]

    def far_spectra(low, high, stage):
        for i in range(low, high):
            far_cut(i, stage)
        found = spectra(far, low, high - low)
        for w, value in enumerate(found):
            far_spec[low * chips + w] = value.astype(BF16)

    def far_centres(low, high):
        many = (high - low) * chips
        crossed = []
        for i in range(low, high):
            day = first_s[0, perm_s[0, i] if fast else i]
            for c in range(chips):
                value = far_spec[i * chips + c]
                crossed.append(spec[day * chips + c] * jnp.concatenate([value, value], axis=1))
        reals, imags = [], []
        for start, size in split(many, 1):
            along = jnp.concatenate(crossed[start:start + size], axis=0)
            along = jnp.dot(along, back[...], preferred_element_type=F32)
            for w in range(size):
                part = along[w * kept:(w + 1) * kept]
                reals.append(part[:, :width])
                imags.append(part[:, width:])
        turned = []
        for start, size in split(many, 1):
            both = []
            for w in range(start, start + size):
                last = crossed[w][nyquist:, :width].astype(F32)[:SMAX] * corner
                last = jnp.sum(last, axis=1, keepdims=True) * corner_wave
                last = last + tile(imags[w], tiles)
                imags[w] = jnp.concatenate(
                    [imags[w][:nyquist], last, imags[w][nyquist + SMAX:]], axis=0
                )
                both.append(imags[w].astype(BF16))
            both = jnp.dot(
                final[...], jnp.concatenate(both, axis=1), preferred_element_type=F32
            )
            turned += [both[:, k * width:(k + 1) * width] for k in range(size)]
        for b in range(high - low):
            for c in range(chips):
                w = b * chips + c
                real, imag, turn = reals[w], imags[w], turned[w]
                energy, tilt, nodes = None, None, None
                for t in range(1, tiles):
                    r, i = tile(real, t), tile(imag, t)
                    square = r * r + i * i
                    energy = square if energy is None else energy + square
                    nodes = r if nodes is None else nodes + r
                for t in range(tiles + 1):
                    cross = tile(real, t) * tile(turn, t)
                    tilt = cross if tilt is None else tilt + cross
                r, i = tile(real, 0), tile(imag, 0)
                energy = energy + r * r * real_weight + i * i * imag_weight
                nodes = 2.0 * nodes + r * edge_weight
                r, i = tile(real, tiles), tile(imag, tiles)
                energy = energy + (r * r + i * i) * 0.25
                nodes = jnp.sum((nodes + r) * flip, axis=0, keepdims=True)
                at = (c, pl.ds(low + b, 1))
                sums[at] = jnp.sum(energy, axis=0, keepdims=True) * (2.0 * width)
                tilt = jnp.sum(tilt, axis=0, keepdims=True)
                moments[at] = tilt - nodes * nodes * (0.5 * length)

    middle = dates // 2
    if fast:
        near_part(0, middle)
        for link, side in ((2, "down"), (4, "up")):
            move.got((link, "now_edge"))
            move.start((6 - link, "relay_edge"))
            move.z_start(side, link)
        move.start((4, "later_rest"), (2, "later_rest"))
        for link, side in ((2, "up"), (4, "down")):
            move.got((link, "later_edge"))
            move.z_start(side, link)
            move.start(("core", link, "edge"))
        near_part(middle, dates)
        for link in (2, 4):
            move.got((link, "now_rest"))
            move.start((6 - link, "relay_rest"), ("core", link, "now"))
        ordered.wait()
        for link, side in ((2, "up"), (4, "down")):
            move.got((link, "relay_edge"))
            move.z_start(side, 6)
            move.start(("core", 6, link, "edge"))
        for k in range(move.inner):
            for link in (2, 4):
                move.got((link, "later_rest", k))
                move.start(("core", link, "rest", k))
        move.got(("core", 0), ("core", 2), ("core", 4))
        for d in (0, 2, 4):
            move.z_got(d)

        def hand_on(*pieces):
            for k in pieces:
                for link in (2, 4):
                    move.got((link, "relay_rest", k))
                    move.start(("core", 6, link, "rest", k))

        early = pairs - 2 * cap
        hand_on(*range(move.inner))
        far_spectra(0, early, 1)
        far_centres(0, early)
        move.got(("core", 6))
        move.z_got(6)
        far_spectra(early, pairs, 2)
        far_centres(early, pairs)
        sent = move.kinds
    else:
        near_part(0, middle)
        near_part(middle, dates)
        plain_gather(n, me, strip, strips, grid, send, recv)
        far_spectra(0, pairs, 1)
        far_centres(0, pairs)
        sent = 2 + 3 * (n - 1)

    across = lax.broadcasted_iota(I32, (pairs, width), 1)
    across = jnp.where(across < length, across, across - width).astype(F32) * 0.5
    cells = 1.0 / (width * width)
    held_columns = columns_v[...]
    lives = held_columns[:, 2 * chips:2 * chips + 1] > 0.5
    spread = spread_v[...]
    found = [None] * (2 * chips)
    for c in range(chips):
        held = sums[c]
        scale = jnp.sum(held, axis=1, keepdims=True) * cells + 1e-6
        low = jnp.sum(moments[c], axis=1, keepdims=True) * cells
        side = jnp.sum(held * across, axis=1, keepdims=True) * cells
        for x, value in enumerate((low, side)):
            k = x * chips + c
            found[k] = jnp.where(lives, held_columns[:, k:k + 1] + value / scale, 0.0)
            partial[k:k + 1] = jnp.sum(found[k] * spread, axis=0, keepdims=True)

    copies = []
    for j in range(1, n):
        where = {"date": lax.rem(me + j, n)}
        copies.append(remote(sent + j - 1, partial, held_sums.at[j - 1], where, send, recv))
        copies[-1].start()
    pick = picked[...]
    for x in range(2):
        for c in range(chips):
            offsets_out[x, c:c + 1] = jnp.sum(found[x * chips + c] * pick, axis=0, keepdims=True)
    if fast:
        move.left()
    total = partial[...]
    for j, copy in enumerate(copies):
        copy.wait_recv()
        total = total + held_sums[j]
    for x in range(2):
        for c in range(chips):
            k = x * chips + c
            value = jnp.sum(inverse[k] * total[k:k + 1], axis=1)[None]
            series_out[x, c:c + 1] = value
    for copy in copies:
        copy.wait_send()


def emit_kernel(offsets, series, offsets_out, series_out, done):
    copies = [
        pltpu.make_async_copy(a, b, done.at[k])
        for k, (a, b) in enumerate(((offsets, offsets_out), (series, series_out)))
    ]
    for copy in copies:
        copy.start()
    for copy in copies:
        copy.wait()


def body(n, strips, images, inverse, first, block, second, count, shifts, anchors):
    dates, length, cols = images.shape
    pairs, chips = first.shape[0], anchors.shape[0]
    vmem, anywhere = pl.BlockSpec(memory_space=pltpu.VMEM), pl.BlockSpec(memory_space=pl.ANY)
    tables = make_tables(length)
    fast = n == 8
    half = length // SMAX // 2
    kinds = (17 + 14 + 8 * PIECES if fast else 2 + 3 * (n - 1)) + n - 1
    width = 2 * length
    cap = 2 * pairs // n
    groups = length // SMAX + 2
    share = inverse.shape[2]
    block_shape = (groups, dates, SMAX, cols)
    late = (2, *block_shape) if fast else (SMAX, cols)
    offsets, series = pl.pallas_call(
        functools.partial(pairs_kernel, n, strips, cap),
        name="pairs",
        out_shape=(
            pltpu.VMEM((2, chips, pairs), F32),
            pltpu.VMEM((2, chips, share), F32),
        ),
        in_specs=[anywhere] * 12,
        out_specs=(vmem, vmem),
        scratch_shapes=[
            pltpu.SMEM((1, pairs), I32),
            pltpu.SMEM((1, pairs), I32),
            pltpu.SMEM((1, pairs), I32),
            pltpu.SMEM((1,), I32),
            pltpu.SMEM((2, chips, pairs), I32),
            pltpu.SMEM((chips,), I32),
            pltpu.SMEM((1, pairs), I32),
            pltpu.VMEM((1, pairs), I32),
            pltpu.VMEM((1, pairs), I32),
            pltpu.VMEM((1, pairs), I32),
            pltpu.VMEM((2, chips, pairs), I32),
            pltpu.VMEM((2 * chips, share, n * dates), F32),
            *[pltpu.VMEM(table.shape, BF16) for table in tables],
            pltpu.VMEM((6 if fast else n, *block_shape), BF16),
            pltpu.VMEM(late, BF16),
            pltpu.VMEM((2 * chips, n * dates), F32),
            pltpu.VMEM((n - 1, 2 * chips, n * dates), F32),
            pltpu.SemaphoreType.DMA((groups + 14,)),
            pltpu.SemaphoreType.DMA((kinds,)),
            pltpu.SemaphoreType.DMA((kinds,)),
            pltpu.VMEM((pairs, length + 2 * SMAX, cols), F32),
            pltpu.VMEM((pairs, length, cols), BF16),
            pltpu.VMEM((dates, length, cols), BF16),
            pltpu.VMEM((dates * chips, tables[1].shape[0], 2 * width), BF16),
            pltpu.VMEM((pairs * chips, tables[1].shape[0], width), BF16),
            pltpu.VMEM((chips, pairs, width), F32),
            pltpu.VMEM((chips, pairs, width), F32),
            pltpu.VMEM((pairs, pairs), F32),
            pltpu.VMEM((pairs, n * dates), F32),
            pltpu.VMEM((pairs, cols), F32),
            pltpu.VMEM((1, pairs), I32),
        ],
        compiler_params=pltpu.CompilerParams(collective_id=0, has_side_effects=True),
    )(
        first.reshape(1, pairs), block.reshape(1, pairs), second.reshape(1, pairs), count,
        jnp.transpose(shifts, (1, 2, 0)), anchors,
        images.reshape(dates, length // SMAX, SMAX, cols),
        inverse.reshape(2 * chips, share, n * dates), *tables,
    )
    offsets, series = pl.pallas_call(
        emit_kernel,
        name="emit",
        out_shape=(
            jax.ShapeDtypeStruct(offsets.shape, F32),
            jax.ShapeDtypeStruct(series.shape, F32),
        ),
        in_specs=[vmem] * 2,
        out_specs=(anywhere, anywhere),
        scratch_shapes=[pltpu.SemaphoreType.DMA((2,))],
    )(
        pltpu.with_memory_space_constraint(offsets, pltpu.VMEM),
        pltpu.with_memory_space_constraint(series, pltpu.VMEM),
    )
    return jnp.transpose(offsets, (2, 0, 1)), series


def solution(mesh):
    return jax.shard_map(
        functools.partial(body, mesh.shape["date"], mesh.shape["strip"]),
        mesh=mesh,
        in_specs=(
            P("date", "strip", None),
            P(None, "strip", "date", None),
            P("date"),
            P("date", None),
            P("date"),
            P("date"),
            P("date", None, "strip"),
            P("strip"),
        ),
        out_specs=(P("date", None, "strip"), P(None, "strip", "date")),
        check_vma=False,
    )
```

```python
import functools
import math

import jax
import jax.numpy as jnp
import numpy as np
from jax import lax
from jax.experimental import pallas as pl
from jax.experimental.pallas import tpu as pltpu
from jax.sharding import PartitionSpec as P

SMAX = 8
SPLIT = 8
PIECES = 1
MESH = pl.DeviceIdType.MESH
F32, BF16, I32 = jnp.float32, jnp.bfloat16, jnp.int32


def make_tables(length):
    counter = np.arange(length)
    radians = (counter[:, None] * counter[None, :] % length) * (2.0 * math.pi / length)
    cosine, sine = np.cos(radians), -np.sin(radians)
    over = 2 * length
    signed = np.where(counter < length // 2, counter, counter - length)
    places = np.arange(over)
    angles = (signed[:, None] * places[None, :] % over) * (2.0 * math.pi / over)
    vcos, vsin = np.cos(angles), np.sin(angles)
    forward = np.concatenate([cosine, sine], axis=1)
    empty = np.zeros_like(forward)
    forward = np.block([[forward, empty], [empty, forward]])
    half = length // 2
    kept = -(-(half + 1) // 16) * 16
    rows = np.zeros((kept, over))
    rows[:half + 1] = np.concatenate([cosine, sine], axis=1)[:half + 1]
    vsin[half] = 0.0
    one = np.concatenate([vcos, vsin], axis=1)
    two = np.concatenate([-vsin, vcos], axis=1)
    back = np.concatenate([one, one, two, -two], axis=0)
    lean = ((places + length) % over - length) * 0.5
    waves = counter[:half + 1, None] * places[None, :] * (2.0 * math.pi / over)
    even = np.where((counter[:half + 1] == 0) | (counter[:half + 1] == half), 1.0, 2.0)
    odd = np.where(counter[:half + 1] == half, 1.0, -2.0)
    final = np.zeros((kept, kept))
    final[:half + 1, :half + 1] = 2.0 * (even[:, None] * np.cos(waves) * lean) @ (
        odd[:, None] * np.sin(waves)
    ).T
    return [jnp.asarray(t.astype(np.float32)).astype(BF16) for t in (forward, rows, back, final)]


def remote(k, src, dst, where, send, recv):
    return pltpu.make_async_remote_copy(
        src_ref=src,
        dst_ref=dst,
        send_sem=send.at[k],
        recv_sem=recv.at[k],
        device_id=where,
        device_id_type=MESH,
    )


class Gather:
    def __init__(self, me, strip, strips, blocks, send, recv):
        self.blocks = blocks
        groups = blocks[0].shape[0]
        half = (groups - 2) // 2
        last = groups - 2
        self.has_up, self.has_down = strip > 0, strip < strips - 1
        up, down = lax.max(strip - 1, 0), lax.min(strip + 1, strips - 1)
        to = {j: jnp.bitwise_xor(me, j) for j in (1, 2, 4)}
        self.to, self.up, self.down = to, up, down
        self.copies = {}
        self.kinds = 0

        def add(name, d, at, many, where, target, dst_at=None):
            dst_at = at if dst_at is None else dst_at
            copy = remote(
                self.kinds,
                blocks[d].at[pl.ds(at, many)],
                blocks[target].at[pl.ds(dst_at, many)],
                where,
                send,
                recv,
            )
            self.copies[name] = copy
            self.kinds += 1

        edges = {"one": 1, "two": last}
        rests = {"one": 2, "two": 1 + half}
        inner = half - 1
        core = {"date": to[1]}
        add(("core", 0), 0, 1, 2 * half, core, 1)
        for link, now, later, relayed in ((4, "one", "two", 2), (2, "two", "one", 4)):
            where = {"date": to[link]}
            add((link, "now_edge"), 0, edges[now], 1, where, link)
            add((link, "now_rest"), 0, rests[now], inner, where, link)
            add((link, "later_edge"), 0, edges[later], 1, where, link)
            add((link, "relay_edge"), relayed, edges[later], 1, where, 6)
            begin = min(edges[now], rests[now])
            add(("core", link, "now"), link, begin, half, core, link ^ 1)
            add(("core", link, "edge"), link, edges[later], 1, core, link ^ 1)
            add(("core", 6, link, "edge"), 6, edges[later], 1, core, 7)
            for k in range(PIECES):
                many = inner // PIECES
                at = rests[later] + k * many
                add((link, "later_rest", k), 0, at, many, where, link)
                add((link, "relay_rest", k), relayed, at, many, where, 6)
                add(("core", link, "rest", k), link, at, many, core, link ^ 1)
                add(("core", 6, link, "rest", k), 6, at, many, core, 7)
        self.inner = PIECES
        for d in (0, 2, 4, 6):
            for flip in (0, 1):
                spot = {"date": jnp.bitwise_xor(me, flip)} if flip else {}
                add(("up", d, flip), d, 1, 1, {"strip": up, **spot}, d ^ flip, groups - 1)
                add(("down", d, flip), d, last, 1, {"strip": down, **spot}, d ^ flip, 0)

    def named(self, names):
        for key, copy in self.copies.items():
            if key in names or key[:2] in names:
                yield copy

    def start(self, *names):
        for copy in self.named(names):
            copy.start()

    def got(self, *names):
        for copy in self.named(names):
            copy.wait_recv()

    def z_start(self, side, d):
        has = self.has_up if side == "up" else self.has_down

        @pl.when(has)
        def _():
            for flip in (0, 1):
                self.copies[(side, d, flip)].start()

    def z_got(self, d, flips=(0, 1)):
        @pl.when(self.has_down)
        def _():
            for flip in flips:
                self.copies[("up", d, flip)].wait_recv()

        @pl.when(self.has_up)
        def _():
            for flip in flips:
                self.copies[("down", d, flip)].wait_recv()

    def left(self):
        for name, copy in self.copies.items():
            if name[0] == "up":
                pl.when(self.has_up)(copy.wait_send)
            elif name[0] == "down":
                pl.when(self.has_down)(copy.wait_send)
            else:
                copy.wait_send()


def plain_gather(n, me, strip, strips, grid, send, recv):
    groups = grid.shape[1]
    has_up, has_down = strip > 0, strip < strips - 1
    up, down = lax.max(strip - 1, 0), lax.min(strip + 1, strips - 1)
    z_up = remote(0, grid.at[me, 1], grid.at[me, groups - 1], {"strip": up}, send, recv)
    z_down = remote(1, grid.at[me, groups - 2], grid.at[me, 0], {"strip": down}, send, recv)
    pl.when(has_up)(z_up.start)
    pl.when(has_down)(z_down.start)
    copies = []
    peers = [{"date": lax.rem(me + j, n)} for j in range(1, n)]
    main = pl.ds(1, groups - 2)
    for j, peer in enumerate(peers):
        part = grid.at[me, main]
        copies.append(remote(2 + j, part, part, peer, send, recv))
        copies[-1].start()
    pl.when(has_down)(z_up.wait_recv)
    pl.when(has_up)(z_down.wait_recv)
    pl.when(has_up)(z_up.wait_send)
    pl.when(has_down)(z_down.wait_send)
    for side, at in ((0, 0), (1, groups - 1)):
        for j, peer in enumerate(peers):
            part = grid.at[me, at]
            copies.append(remote(2 + (1 + side) * (n - 1) + j, part, part, peer, send, recv))
            copies[-1].start()
    for copy in copies:
        copy.wait()


def pairs_kernel(
    n, strips, cap,
    first_h, block_h, second_h, count_h, shifts_h, anchors_h,
    img, inverse_h, forward_h, rows_h, back_h, final_h,
    offsets_out, series_out,
    first_s, block_s, second_s, count_s, shifts_s, anchors_s, perm_s,
    first_v, block_v, second_v, shifts_v, inverse, forward, rows, back, final,
    grid, late, partial, held_sums,
    local, send, recv,
    wide, spec, far_spec, sums, moments, picked, spread_v, columns_v, perm_v,
):
    groups, dates, _, cols = grid.shape[1:]
    length = SMAX * (groups - 2)
    pairs, chips = first_s.shape[1], anchors_s.shape[0]
    fast = n == 8
    me, strip = lax.axis_index("date"), lax.axis_index("strip")
    has_up, has_down = strip > 0, strip < strips - 1
    up, down = lax.max(strip - 1, 0), lax.min(strip + 1, strips - 1)

    barrier = pltpu.get_barrier_semaphore()
    if fast:
        greeted = [{"date": jnp.bitwise_xor(me, j)} for j in (1, 2, 4)]
        side_spots = [{}, {"date": jnp.bitwise_xor(me, 1)}]
    else:
        greeted = [{"date": lax.rem(me + j, n)} for j in range(1, n)]
        side_spots = [{}]
    for where in greeted:
        pl.semaphore_signal(barrier, inc=1, device_id=where, device_id_type=MESH)
    for other, has in ((up, has_up), (down, has_down)):
        @pl.when(has)
        def _():
            for spot in side_spots:
                pl.semaphore_signal(
                    barrier, inc=1, device_id={"strip": other, **spot}, device_id_type=MESH
                )

    count = iter(range(local.shape[0]))

    def load(src, dst):
        copy = pltpu.make_async_copy(src, dst, local.at[next(count)])
        copy.start()
        return copy

    own = 0 if fast else me
    spots = [0, groups - 3, *range(1, groups - 3)]
    mine = [load(img.at[:, g], grid.at[own, 1 + g]) for g in spots]
    small = [
        load(a, b)
        for a, b in (
            (first_h, first_s), (block_h, block_s), (second_h, second_s), (count_h, count_s),
            (shifts_h, shifts_s), (anchors_h, anchors_s),
            (first_h, first_v), (block_h, block_v), (second_h, second_v), (shifts_h, shifts_v),
        )
    ]
    large = [
        load(a, b)
        for a, b in (
            (forward_h, forward), (rows_h, rows), (back_h, back), (final_h, final),
            (inverse_h, inverse),
        )
    ]
    sides = len(side_spots) * (has_up.astype(I32) + has_down.astype(I32))
    pl.semaphore_wait(barrier, len(greeted) + sides)
    for copy in mine[:2]:
        copy.wait()
    if fast:
        blocks = [grid.at[d] for d in range(6)] + [late.at[d] for d in range(2)]
        move = Gather(me, strip, strips, blocks, send, recv)
        move.start((4, "now_edge"), (2, "now_edge"))
        move.start((4, "later_edge"), (2, "later_edge"))
        move.z_start("up", 0)
        move.z_start("down", 0)
    for copy in mine[2:]:
        copy.wait()
    if fast:
        move.start((4, "now_rest"), (2, "now_rest"), ("core", 0))
    for copy in small + large:
        copy.wait()

    line = lax.broadcasted_iota(I32, (pairs, pairs), 0)
    place = lax.broadcasted_iota(I32, (pairs, pairs), 1)
    if fast:
        distance = jnp.bitwise_xor(block_v[...], me)
        key = jnp.broadcast_to(jnp.maximum(distance - 5, 0), (pairs, pairs))
        key_line = jnp.sum(jnp.where(line == place, key, 0), axis=1, keepdims=True)
        ahead = (key < key_line) | ((key == key_line) & (place < line))
        rank_line = jnp.sum(ahead.astype(I32), axis=1, keepdims=True)
        behind = (key_line < key) | ((key_line == key) & (line < place))
        rank = jnp.sum(behind.astype(I32), axis=0, keepdims=True)
        perm_v[...] = jnp.sum(jnp.where(rank_line == place, line, 0), axis=0, keepdims=True)
        ordered = load(perm_v, perm_s)
        pick = (jnp.broadcast_to(rank, (pairs, pairs)) == line).astype(F32)
    else:
        pick = (line == place).astype(F32)
    picked[...] = pick

    def chosen(row):
        return jnp.sum(pick * row, axis=1, keepdims=True)

    spot = lax.broadcasted_iota(I32, (pairs, partial.shape[1]), 1).astype(F32)
    to_date = chosen((block_v[...] * dates + second_v[...]).astype(F32))
    from_date = chosen((me * dates + first_v[...]).astype(F32))
    spread_v[...] = (spot == to_date).astype(F32) - (spot == from_date).astype(F32)
    live = (lax.broadcasted_iota(I32, (1, pairs), 1) < count_s[0]).astype(F32)
    at = lax.broadcasted_iota(I32, columns_v.shape, 1)
    held_columns = jnp.where(at == 2 * chips, chosen(live), 0.0)
    for x in range(2):
        for c in range(chips):
            column = chosen(shifts_v[x, c:c + 1].astype(F32))
            held_columns = jnp.where(at == x * chips + c, column, held_columns)
    columns_v[...] = held_columns

    lane = lax.broadcasted_iota(I32, (1, cols), 1)
    left_half = lane < length

    def paired(one, start_one, two, start_two):
        one = pltpu.roll(one.astype(BF16), lax.rem(2 * cols - start_one, cols), 1)
        two = pltpu.roll(two.astype(BF16), lax.rem(2 * cols + length - start_two, cols), 1)
        column = jnp.where(left_half, start_one + lane, start_two - length + lane)
        inside = (column >= 0) & (column < cols)
        keep_one = jnp.where(left_half & inside, 1.0, 0.0).astype(BF16)
        keep_two = jnp.where(left_half, 0.0, jnp.where(inside, 1.0, 0.0)).astype(BF16)
        return one * keep_one + two * keep_two

    width = 2 * length
    lanes2 = lax.broadcasted_iota(I32, (1, 2 * width), 1)
    base = jnp.where((lanes2 == 0) | (lanes2 == width), 1.0 / length, 0.0)
    turn_sign = jnp.where(left_half, -1.0, 1.0).astype(BF16)

    def split(many, size):
        step = max(1, many // SPLIT) * size
        return [(at, step) for at in range(0, many * size, step)]

    def spectra(windows):
        many = len(windows)
        sections = []
        for start, size in split(many, length):
            some = windows[start // length:(start + size) // length]
            found = jnp.dot(
                jnp.concatenate(some, axis=0), forward[...], preferred_element_type=F32
            )
            sections += [found[k:k + length] for k in range(0, size, length)]
        stacked = []
        for part in sections:
            part = part - jnp.sum(part, axis=0, keepdims=True) * base
            for c in range(2):
                top = part[:, c * width:(c + 1) * width]
                top = top.astype(BF16)
                low = pltpu.roll(top, length, 1) * turn_sign
                stacked.append(jnp.concatenate([top, low], axis=0))
        found = []
        for start, size in split(many, 2):
            both = jnp.concatenate(stacked[start:start + size], axis=1)
            both = jnp.dot(rows[...], both, preferred_element_type=F32)
            found += [both[:, k * width:(k + 1) * width] for k in range(size)]
        return found

    def near_part(low, high):
        windows = []
        for d in range(low, high):
            value = grid[own, pl.ds(1, groups - 2), d].astype(F32).reshape(length, cols)
            windows.append(paired(value, anchors_s[0], value, anchors_s[1]))
        found = spectra(windows)
        for w in range((high - low) * chips):
            both = jnp.concatenate([found[w], pltpu.roll(found[w], length, 1)], axis=1)
            spec[low * chips + w] = both.astype(BF16)

    def far_cut(i, stage):
        p = perm_s[0, i] if fast else i
        block, day = block_s[0, p], second_s[0, p]
        if fast:
            distance = jnp.bitwise_xor(block, me)
            value = grid[jnp.where(distance < 6, distance, 0), :, day]
            if stage > 1:
                other = late[jnp.where(distance == 7, 1, 0), :, day]
                value = jnp.where(distance < 6, value, other)
            value = value.astype(F32)
        else:
            value = grid[block, :, day].astype(F32)
        wide[i, pl.ds(0, SMAX)] = jnp.where(has_up, value[0], 0.0)
        wide[i, pl.ds(SMAX, length)] = value[1:groups - 1].reshape(length, cols)
        wide[i, pl.ds(SMAX + length, SMAX)] = jnp.where(has_down, value[groups - 1], 0.0)
        windows = []
        for c in range(2):
            windows.append(wide[i, pl.ds(SMAX + shifts_s[0, c, p], length)])
            windows.append(anchors_s[c] + shifts_s[1, c, p])
        return paired(*windows)

    kept, nyquist = rows.shape[0], length // 2
    tiles = nyquist // SMAX
    row_in = lax.broadcasted_iota(I32, (SMAX, width), 0)
    lane_in = lax.broadcasted_iota(I32, (SMAX, width), 1)
    top = row_in == 0
    real_weight, imag_weight = jnp.where(top, 0.5, 1.0), jnp.where(top, 0.0, 1.0)
    edge_weight, flip = jnp.where(top, 1.0, 2.0), jnp.where(lax.rem(row_in, 2) == 0, 1.0, -1.0)
    corner = jnp.where(top & (lax.rem(lane_in, length) == nyquist), 1.0, 0.0)
    quarter = lax.rem(lane_in, 4)
    corner_wave = jnp.where(quarter == 1, -1.0, jnp.where(quarter == 3, 1.0, 0.0))

    def tile(value, t):
        return value[t * SMAX:(t + 1) * SMAX]

    def far_spectra(low, high, stage):
        found = spectra([far_cut(i, stage) for i in range(low, high)])
        for w, value in enumerate(found):
            far_spec[low * chips + w] = value.astype(BF16)

    def far_centres(low, high):
        many = (high - low) * chips
        crossed = []
        for i in range(low, high):
            day = first_s[0, perm_s[0, i] if fast else i]
            for c in range(chips):
                value = far_spec[i * chips + c]
                crossed.append(spec[day * chips + c] * jnp.concatenate([value, value], axis=1))
        reals, imags = [], []
        for start, size in split(many, 1):
            along = jnp.concatenate(crossed[start:start + size], axis=0)
            along = jnp.dot(along, back[...], preferred_element_type=F32)
            for w in range(size):
                part = along[w * kept:(w + 1) * kept]
                reals.append(part[:, :width])
                imags.append(part[:, width:])
        turned = []
        for start, size in split(many, 1):
            both = []
            for w in range(start, start + size):
                last = crossed[w][nyquist:, :width].astype(F32)[:SMAX] * corner
                last = jnp.sum(last, axis=1, keepdims=True) * corner_wave
                last = last + tile(imags[w], tiles)
                imags[w] = jnp.concatenate(
                    [imags[w][:nyquist], last, imags[w][nyquist + SMAX:]], axis=0
                )
                both.append(imags[w].astype(BF16))
            both = jnp.dot(
                final[...], jnp.concatenate(both, axis=1), preferred_element_type=F32
            )
            turned += [both[:, k * width:(k + 1) * width] for k in range(size)]
        for b in range(high - low):
            for c in range(chips):
                w = b * chips + c
                real, imag, turn = reals[w], imags[w], turned[w]
                energy, tilt, nodes = None, None, None
                for t in range(1, tiles):
                    r, i = tile(real, t), tile(imag, t)
                    square = r * r + i * i
                    energy = square if energy is None else energy + square
                    nodes = r if nodes is None else nodes + r
                for t in range(tiles + 1):
                    cross = tile(real, t) * tile(turn, t)
                    tilt = cross if tilt is None else tilt + cross
                r, i = tile(real, 0), tile(imag, 0)
                energy = energy + r * r * real_weight + i * i * imag_weight
                nodes = 2.0 * nodes + r * edge_weight
                r, i = tile(real, tiles), tile(imag, tiles)
                energy = energy + (r * r + i * i) * 0.25
                nodes = jnp.sum((nodes + r) * flip, axis=0, keepdims=True)
                at = (c, pl.ds(low + b, 1))
                sums[at] = jnp.sum(energy, axis=0, keepdims=True) * (2.0 * width)
                tilt = jnp.sum(tilt, axis=0, keepdims=True)
                moments[at] = tilt - nodes * nodes * (0.5 * length)

    middle = dates // 2
    if fast:
        near_part(0, middle)
        for link, side in ((2, "down"), (4, "up")):
            move.got((link, "now_edge"))
            move.start((6 - link, "relay_edge"))
            move.z_start(side, link)
        move.start((4, "later_rest"), (2, "later_rest"))
        for link, side in ((2, "up"), (4, "down")):
            move.got((link, "later_edge"))
            move.z_start(side, link)
            move.start(("core", link, "edge"))
        near_part(middle, dates)
        for link in (2, 4):
            move.got((link, "now_rest"))
            move.start((6 - link, "relay_rest"), ("core", link, "now"))
        ordered.wait()
        for link, side in ((2, "up"), (4, "down")):
            move.got((link, "relay_edge"))
            move.z_start(side, 6)
            move.start(("core", 6, link, "edge"))
        for k in range(move.inner):
            for link in (2, 4):
                move.got((link, "later_rest", k))
                move.start(("core", link, "rest", k))
        move.got(("core", 0), ("core", 2), ("core", 4))
        for d in (0, 2, 4):
            move.z_got(d)

        def hand_on(*pieces):
            for k in pieces:
                for link in (2, 4):
                    move.got((link, "relay_rest", k))
                    move.start(("core", 6, link, "rest", k))

        early = pairs - 2 * cap
        hand_on(*range(move.inner))
        far_spectra(0, early, 1)
        far_centres(0, early)
        move.got(("core", 6))
        move.z_got(6)
        far_spectra(early, pairs, 2)
        far_centres(early, pairs)
        sent = move.kinds
    else:
        near_part(0, middle)
        near_part(middle, dates)
        plain_gather(n, me, strip, strips, grid, send, recv)
        far_spectra(0, pairs, 1)
        far_centres(0, pairs)
        sent = 2 + 3 * (n - 1)

    across = lax.broadcasted_iota(I32, (pairs, width), 1)
    across = jnp.where(across < length, across, across - width).astype(F32) * 0.5
    cells = 1.0 / (width * width)
    held_columns = columns_v[...]
    lives = held_columns[:, 2 * chips:2 * chips + 1] > 0.5
    spread = spread_v[...]
    found = [None] * (2 * chips)
    for c in range(chips):
        held = sums[c]
        scale = jnp.sum(held, axis=1, keepdims=True) * cells + 1e-6
        low = jnp.sum(moments[c], axis=1, keepdims=True) * cells
        side = jnp.sum(held * across, axis=1, keepdims=True) * cells
        for x, value in enumerate((low, side)):
            k = x * chips + c
            found[k] = jnp.where(lives, held_columns[:, k:k + 1] + value / scale, 0.0)
            partial[k:k + 1] = jnp.sum(found[k] * spread, axis=0, keepdims=True)

    copies = []
    for j in range(1, n):
        where = {"date": lax.rem(me + j, n)}
        copies.append(remote(sent + j - 1, partial, held_sums.at[j - 1], where, send, recv))
        copies[-1].start()
    pick = picked[...]
    for x in range(2):
        for c in range(chips):
            offsets_out[x, c:c + 1] = jnp.sum(found[x * chips + c] * pick, axis=0, keepdims=True)
    if fast:
        move.left()
    total = partial[...]
    for j, copy in enumerate(copies):
        copy.wait_recv()
        total = total + held_sums[j]
    for x in range(2):
        for c in range(chips):
            k = x * chips + c
            value = jnp.sum(inverse[k] * total[k:k + 1], axis=1)[None]
            series_out[x, c:c + 1] = value
    for copy in copies:
        copy.wait_send()


def emit_kernel(offsets, series, offsets_out, series_out, done):
    copies = [
        pltpu.make_async_copy(a, b, done.at[k])
        for k, (a, b) in enumerate(((offsets, offsets_out), (series, series_out)))
    ]
    for copy in copies:
        copy.start()
    for copy in copies:
        copy.wait()


def body(n, strips, images, inverse, first, block, second, count, shifts, anchors):
    dates, length, cols = images.shape
    pairs, chips = first.shape[0], anchors.shape[0]
    vmem, anywhere = pl.BlockSpec(memory_space=pltpu.VMEM), pl.BlockSpec(memory_space=pl.ANY)
    tables = make_tables(length)
    fast = n == 8
    half = length // SMAX // 2
    kinds = (17 + 14 + 8 * PIECES if fast else 2 + 3 * (n - 1)) + n - 1
    width = 2 * length
    cap = 2 * pairs // n
    groups = length // SMAX + 2
    share = inverse.shape[2]
    block_shape = (groups, dates, SMAX, cols)
    late = (2, *block_shape) if fast else (SMAX, cols)
    offsets, series = pl.pallas_call(
        functools.partial(pairs_kernel, n, strips, cap),
        name="pairs",
        out_shape=(
            pltpu.VMEM((2, chips, pairs), F32),
            pltpu.VMEM((2, chips, share), F32),
        ),
        in_specs=[anywhere] * 12,
        out_specs=(vmem, vmem),
        scratch_shapes=[
            pltpu.SMEM((1, pairs), I32),
            pltpu.SMEM((1, pairs), I32),
            pltpu.SMEM((1, pairs), I32),
            pltpu.SMEM((1,), I32),
            pltpu.SMEM((2, chips, pairs), I32),
            pltpu.SMEM((chips,), I32),
            pltpu.SMEM((1, pairs), I32),
            pltpu.VMEM((1, pairs), I32),
            pltpu.VMEM((1, pairs), I32),
            pltpu.VMEM((1, pairs), I32),
            pltpu.VMEM((2, chips, pairs), I32),
            pltpu.VMEM((2 * chips, share, n * dates), F32),
            *[pltpu.VMEM(table.shape, BF16) for table in tables],
            pltpu.VMEM((6 if fast else n, *block_shape), BF16),
            pltpu.VMEM(late, BF16),
            pltpu.VMEM((2 * chips, n * dates), F32),
            pltpu.VMEM((n - 1, 2 * chips, n * dates), F32),
            pltpu.SemaphoreType.DMA((groups + 14,)),
            pltpu.SemaphoreType.DMA((kinds,)),
            pltpu.SemaphoreType.DMA((kinds,)),
            pltpu.VMEM((pairs, length + 2 * SMAX, cols), F32),
            pltpu.VMEM((dates * chips, tables[1].shape[0], 2 * width), BF16),
            pltpu.VMEM((pairs * chips, tables[1].shape[0], width), BF16),
            pltpu.VMEM((chips, pairs, width), F32),
            pltpu.VMEM((chips, pairs, width), F32),
            pltpu.VMEM((pairs, pairs), F32),
            pltpu.VMEM((pairs, n * dates), F32),
            pltpu.VMEM((pairs, cols), F32),
            pltpu.VMEM((1, pairs), I32),
        ],
        compiler_params=pltpu.CompilerParams(collective_id=0, has_side_effects=True),
    )(
        first.reshape(1, pairs), block.reshape(1, pairs), second.reshape(1, pairs), count,
        jnp.transpose(shifts, (1, 2, 0)), anchors,
        images.reshape(dates, length // SMAX, SMAX, cols),
        inverse.reshape(2 * chips, share, n * dates), *tables,
    )
    offsets, series = pl.pallas_call(
        emit_kernel,
        name="emit",
        out_shape=(
            jax.ShapeDtypeStruct(offsets.shape, F32),
            jax.ShapeDtypeStruct(series.shape, F32),
        ),
        in_specs=[vmem] * 2,
        out_specs=(anywhere, anywhere),
        scratch_shapes=[pltpu.SemaphoreType.DMA((2,))],
    )(
        pltpu.with_memory_space_constraint(offsets, pltpu.VMEM),
        pltpu.with_memory_space_constraint(series, pltpu.VMEM),
    )
    return jnp.transpose(offsets, (2, 0, 1)), series


def solution(mesh):
    return jax.shard_map(
        functools.partial(body, mesh.shape["date"], mesh.shape["strip"]),
        mesh=mesh,
        in_specs=(
            P("date", "strip", None),
            P(None, "strip", "date", None),
            P("date"),
            P("date", None),
            P("date"),
            P("date"),
            P("date", None, "strip"),
            P("strip"),
        ),
        out_specs=(P("date", None, "strip"), P(None, "strip", "date")),
        check_vma=False,
    )
```

```python
import functools
import math

import jax
import jax.numpy as jnp
import numpy as np
from jax import lax
from jax.experimental import pallas as pl
from jax.experimental.pallas import tpu as pltpu
from jax.sharding import PartitionSpec as P

SMAX = 8
SPLIT = 8
PIECES = 1
MESH = pl.DeviceIdType.MESH
F32, BF16, I32 = jnp.float32, jnp.bfloat16, jnp.int32


def make_tables(length):
    counter = np.arange(length)
    radians = (counter[:, None] * counter[None, :] % length) * (2.0 * math.pi / length)
    cosine, sine = np.cos(radians), -np.sin(radians)
    over = 2 * length
    signed = np.where(counter < length // 2, counter, counter - length)
    places = np.arange(over)
    angles = (signed[:, None] * places[None, :] % over) * (2.0 * math.pi / over)
    vcos, vsin = np.cos(angles), np.sin(angles)
    forward = np.concatenate([cosine, sine], axis=1)
    empty = np.zeros_like(forward)
    forward = np.block([[forward, empty], [empty, forward]])
    half = length // 2
    kept = -(-(half + 1) // 16) * 16
    rows = np.zeros((kept, over))
    rows[:half + 1] = np.concatenate([cosine, sine], axis=1)[:half + 1]
    vsin[half] = 0.0
    one = np.concatenate([vcos, vsin], axis=1)
    two = np.concatenate([-vsin, vcos], axis=1)
    back = np.concatenate([one, one, two, -two], axis=0)
    lean = ((places + length) % over - length) * 0.5
    waves = counter[:half + 1, None] * places[None, :] * (2.0 * math.pi / over)
    even = np.where((counter[:half + 1] == 0) | (counter[:half + 1] == half), 1.0, 2.0)
    odd = np.where(counter[:half + 1] == half, 1.0, -2.0)
    final = np.zeros((kept, kept))
    final[:half + 1, :half + 1] = 2.0 * (even[:, None] * np.cos(waves) * lean) @ (
        odd[:, None] * np.sin(waves)
    ).T
    return [jnp.asarray(t.astype(np.float32)).astype(BF16) for t in (forward, rows, back, final)]


def remote(k, src, dst, where, send, recv):
    return pltpu.make_async_remote_copy(
        src_ref=src,
        dst_ref=dst,
        send_sem=send.at[k],
        recv_sem=recv.at[k],
        device_id=where,
        device_id_type=MESH,
    )


class Gather:
    def __init__(self, me, strip, strips, blocks, send, recv):
        self.blocks = blocks
        groups = blocks[0].shape[0]
        half = (groups - 2) // 2
        last = groups - 2
        self.has_up, self.has_down = strip > 0, strip < strips - 1
        up, down = lax.max(strip - 1, 0), lax.min(strip + 1, strips - 1)
        to = {j: jnp.bitwise_xor(me, j) for j in (1, 2, 4)}
        self.to, self.up, self.down = to, up, down
        self.copies = {}
        self.kinds = 0

        def add(name, d, at, many, where, target, dst_at=None):
            dst_at = at if dst_at is None else dst_at
            copy = remote(
                self.kinds,
                blocks[d].at[pl.ds(at, many)],
                blocks[target].at[pl.ds(dst_at, many)],
                where,
                send,
                recv,
            )
            self.copies[name] = copy
            self.kinds += 1

        edges = {"one": 1, "two": last}
        rests = {"one": 2, "two": 1 + half}
        inner = half - 1
        core = {"date": to[1]}
        add(("core", 0), 0, 1, 2 * half, core, 1)
        for link, now, later, relayed in ((4, "one", "two", 2), (2, "two", "one", 4)):
            where = {"date": to[link]}
            add((link, "now_edge"), 0, edges[now], 1, where, link)
            add((link, "now_rest"), 0, rests[now], inner, where, link)
            add((link, "later_edge"), 0, edges[later], 1, where, link)
            add((link, "relay_edge"), relayed, edges[later], 1, where, 6)
            begin = min(edges[now], rests[now])
            add(("core", link, "now"), link, begin, half, core, link ^ 1)
            add(("core", link, "edge"), link, edges[later], 1, core, link ^ 1)
            add(("core", 6, link, "edge"), 6, edges[later], 1, core, 7)
            for k in range(PIECES):
                many = inner // PIECES
                at = rests[later] + k * many
                add((link, "later_rest", k), 0, at, many, where, link)
                add((link, "relay_rest", k), relayed, at, many, where, 6)
                add(("core", link, "rest", k), link, at, many, core, link ^ 1)
                add(("core", 6, link, "rest", k), 6, at, many, core, 7)
        self.inner = PIECES
        for d in (0, 2, 4, 6):
            for flip in (0, 1):
                spot = {"date": jnp.bitwise_xor(me, flip)} if flip else {}
                add(("up", d, flip), d, 1, 1, {"strip": up, **spot}, d ^ flip, groups - 1)
                add(("down", d, flip), d, last, 1, {"strip": down, **spot}, d ^ flip, 0)

    def named(self, names):
        for key, copy in self.copies.items():
            if key in names or key[:2] in names:
                yield copy

    def start(self, *names):
        for copy in self.named(names):
            copy.start()

    def got(self, *names):
        for copy in self.named(names):
            copy.wait_recv()

    def z_start(self, side, d):
        has = self.has_up if side == "up" else self.has_down

        @pl.when(has)
        def _():
            for flip in (0, 1):
                self.copies[(side, d, flip)].start()

    def z_got(self, d, flips=(0, 1)):
        @pl.when(self.has_down)
        def _():
            for flip in flips:
                self.copies[("up", d, flip)].wait_recv()

        @pl.when(self.has_up)
        def _():
            for flip in flips:
                self.copies[("down", d, flip)].wait_recv()

    def left(self):
        for name, copy in self.copies.items():
            if name[0] == "up":
                pl.when(self.has_up)(copy.wait_send)
            elif name[0] == "down":
                pl.when(self.has_down)(copy.wait_send)
            else:
                copy.wait_send()


def plain_gather(n, me, strip, strips, grid, send, recv):
    groups = grid.shape[1]
    has_up, has_down = strip > 0, strip < strips - 1
    up, down = lax.max(strip - 1, 0), lax.min(strip + 1, strips - 1)
    z_up = remote(0, grid.at[me, 1], grid.at[me, groups - 1], {"strip": up}, send, recv)
    z_down = remote(1, grid.at[me, groups - 2], grid.at[me, 0], {"strip": down}, send, recv)
    pl.when(has_up)(z_up.start)
    pl.when(has_down)(z_down.start)
    copies = []
    peers = [{"date": lax.rem(me + j, n)} for j in range(1, n)]
    main = pl.ds(1, groups - 2)
    for j, peer in enumerate(peers):
        part = grid.at[me, main]
        copies.append(remote(2 + j, part, part, peer, send, recv))
        copies[-1].start()
    pl.when(has_down)(z_up.wait_recv)
    pl.when(has_up)(z_down.wait_recv)
    pl.when(has_up)(z_up.wait_send)
    pl.when(has_down)(z_down.wait_send)
    for side, at in ((0, 0), (1, groups - 1)):
        for j, peer in enumerate(peers):
            part = grid.at[me, at]
            copies.append(remote(2 + (1 + side) * (n - 1) + j, part, part, peer, send, recv))
            copies[-1].start()
    for copy in copies:
        copy.wait()


def pairs_kernel(
    n, strips, cap,
    first_h, block_h, second_h, count_h, shifts_h, anchors_h,
    img, inverse_h, forward_h, rows_h, back_h, final_h,
    offsets_out, series_out,
    first_s, block_s, second_s, count_s, shifts_s, anchors_s, perm_s,
    first_v, block_v, second_v, shifts_v, inverse, forward, rows, back, final,
    grid, late, partial, held_sums,
    local, send, recv,
    wide, spec, far_spec, sums, moments, picked, spread_v, columns_v, perm_v,
):
    groups, dates, _, cols = grid.shape[1:]
    length = SMAX * (groups - 2)
    pairs, chips = first_s.shape[1], anchors_s.shape[0]
    fast = n == 8
    me, strip = lax.axis_index("date"), lax.axis_index("strip")
    has_up, has_down = strip > 0, strip < strips - 1
    up, down = lax.max(strip - 1, 0), lax.min(strip + 1, strips - 1)

    barrier = pltpu.get_barrier_semaphore()
    if fast:
        greeted = [{"date": jnp.bitwise_xor(me, j)} for j in (1, 2, 4)]
        side_spots = [{}, {"date": jnp.bitwise_xor(me, 1)}]
    else:
        greeted = [{"date": lax.rem(me + j, n)} for j in range(1, n)]
        side_spots = [{}]
    for where in greeted:
        pl.semaphore_signal(barrier, inc=1, device_id=where, device_id_type=MESH)
    for other, has in ((up, has_up), (down, has_down)):
        @pl.when(has)
        def _():
            for spot in side_spots:
                pl.semaphore_signal(
                    barrier, inc=1, device_id={"strip": other, **spot}, device_id_type=MESH
                )

    count = iter(range(local.shape[0]))

    def load(src, dst):
        copy = pltpu.make_async_copy(src, dst, local.at[next(count)])
        copy.start()
        return copy

    own = 0 if fast else me
    spots = [0, groups - 3, *range(1, groups - 3)]
    mine = [load(img.at[:, g], grid.at[own, 1 + g]) for g in spots]
    small = [
        load(a, b)
        for a, b in (
            (first_h, first_s), (block_h, block_s), (second_h, second_s), (count_h, count_s),
            (shifts_h, shifts_s), (anchors_h, anchors_s),
            (first_h, first_v), (block_h, block_v), (second_h, second_v), (shifts_h, shifts_v),
        )
    ]
    large = [
        load(a, b)
        for a, b in (
            (forward_h, forward), (rows_h, rows), (back_h, back), (final_h, final),
            (inverse_h, inverse),
        )
    ]
    sides = len(side_spots) * (has_up.astype(I32) + has_down.astype(I32))
    pl.semaphore_wait(barrier, len(greeted) + sides)
    for copy in mine[:2]:
        copy.wait()
    if fast:
        blocks = [grid.at[d] for d in range(6)] + [late.at[d] for d in range(2)]
        move = Gather(me, strip, strips, blocks, send, recv)
        move.start((4, "now_edge"), (2, "now_edge"))
        move.start((4, "later_edge"), (2, "later_edge"))
        move.z_start("up", 0)
        move.z_start("down", 0)
    for copy in mine[2:]:
        copy.wait()
    if fast:
        move.start((4, "now_rest"), (2, "now_rest"), ("core", 0))
    for copy in small + large:
        copy.wait()

    line = lax.broadcasted_iota(I32, (pairs, pairs), 0)
    place = lax.broadcasted_iota(I32, (pairs, pairs), 1)
    if fast:
        distance = jnp.bitwise_xor(block_v[...], me)
        key = jnp.broadcast_to(jnp.maximum(distance - 5, 0), (pairs, pairs))
        key_line = jnp.sum(jnp.where(line == place, key, 0), axis=1, keepdims=True)
        ahead = (key < key_line) | ((key == key_line) & (place < line))
        rank_line = jnp.sum(ahead.astype(I32), axis=1, keepdims=True)
        behind = (key_line < key) | ((key_line == key) & (line < place))
        rank = jnp.sum(behind.astype(I32), axis=0, keepdims=True)
        perm_v[...] = jnp.sum(jnp.where(rank_line == place, line, 0), axis=0, keepdims=True)
        ordered = load(perm_v, perm_s)
        pick = (jnp.broadcast_to(rank, (pairs, pairs)) == line).astype(F32)
    else:
        pick = (line == place).astype(F32)
    picked[...] = pick

    def chosen(row):
        return jnp.sum(pick * row, axis=1, keepdims=True)

    spot = lax.broadcasted_iota(I32, (pairs, partial.shape[1]), 1).astype(F32)
    to_date = chosen((block_v[...] * dates + second_v[...]).astype(F32))
    from_date = chosen((me * dates + first_v[...]).astype(F32))
    spread_v[...] = (spot == to_date).astype(F32) - (spot == from_date).astype(F32)
    live = (lax.broadcasted_iota(I32, (1, pairs), 1) < count_s[0]).astype(F32)
    at = lax.broadcasted_iota(I32, columns_v.shape, 1)
    held_columns = jnp.where(at == 2 * chips, chosen(live), 0.0)
    for x in range(2):
        for c in range(chips):
            column = chosen(shifts_v[x, c:c + 1].astype(F32))
            held_columns = jnp.where(at == x * chips + c, column, held_columns)
    columns_v[...] = held_columns

    lane = lax.broadcasted_iota(I32, (1, cols), 1)
    left_half = lane < length

    def paired(one, start_one, two, start_two):
        one = pltpu.roll(one.astype(BF16), lax.rem(2 * cols - start_one, cols), 1)
        two = pltpu.roll(two.astype(BF16), lax.rem(2 * cols + length - start_two, cols), 1)
        column = jnp.where(left_half, start_one + lane, start_two - length + lane)
        inside = (column >= 0) & (column < cols)
        keep_one = jnp.where(left_half & inside, 1.0, 0.0).astype(BF16)
        keep_two = jnp.where(left_half, 0.0, jnp.where(inside, 1.0, 0.0)).astype(BF16)
        return one * keep_one + two * keep_two

    width = 2 * length
    lanes2 = lax.broadcasted_iota(I32, (1, 2 * width), 1)
    base = jnp.where((lanes2 == 0) | (lanes2 == width), 1.0 / length, 0.0)
    turn_sign = jnp.where(left_half, -1.0, 1.0).astype(BF16)

    def split(many, size):
        step = max(1, many // SPLIT) * size
        return [(at, step) for at in range(0, many * size, step)]

    def spectra(windows):
        many = len(windows)
        sections = []
        for start, size in split(many, length):
            some = windows[start // length:(start + size) // length]
            found = jnp.dot(
                jnp.concatenate(some, axis=0), forward[...], preferred_element_type=F32
            )
            sections += [found[k:k + length] for k in range(0, size, length)]
        stacked = []
        for part in sections:
            part = part - jnp.sum(part, axis=0, keepdims=True) * base
            for c in range(2):
                top = part[:, c * width:(c + 1) * width]
                top = top.astype(BF16)
                low = pltpu.roll(top, length, 1) * turn_sign
                stacked.append(jnp.concatenate([top, low], axis=0))
        found = []
        for start, size in split(many, 2):
            both = jnp.concatenate(stacked[start:start + size], axis=1)
            both = jnp.dot(rows[...], both, preferred_element_type=F32)
            found += [both[:, k * width:(k + 1) * width] for k in range(size)]
        return found

    def near_part(low, high):
        windows = []
        for d in range(low, high):
            value = grid[own, pl.ds(1, groups - 2), d].astype(F32).reshape(length, cols)
            windows.append(paired(value, anchors_s[0], value, anchors_s[1]))
        found = spectra(windows)
        for w in range((high - low) * chips):
            both = jnp.concatenate([found[w], pltpu.roll(found[w], length, 1)], axis=1)
            spec[low * chips + w] = both.astype(BF16)

    def far_cut(i, stage):
        p = perm_s[0, i] if fast else i
        block, day = block_s[0, p], second_s[0, p]
        if fast:
            distance = jnp.bitwise_xor(block, me)
            value = grid[jnp.where(distance < 6, distance, 0), :, day]
            if stage > 1:
                other = late[jnp.where(distance == 7, 1, 0), :, day]
                value = jnp.where(distance < 6, value, other)
            value = value.astype(F32)
        else:
            value = grid[block, :, day].astype(F32)
        wide[i, pl.ds(0, SMAX)] = jnp.where(has_up, value[0], 0.0)
        wide[i, pl.ds(SMAX, length)] = value[1:groups - 1].reshape(length, cols)
        wide[i, pl.ds(SMAX + length, SMAX)] = jnp.where(has_down, value[groups - 1], 0.0)
        windows = []
        for c in range(2):
            windows.append(wide[i, pl.ds(SMAX + shifts_s[0, c, p], length)])
            windows.append(anchors_s[c] + shifts_s[1, c, p])
        return paired(*windows)

    kept, nyquist = rows.shape[0], length // 2
    tiles = nyquist // SMAX
    row_in = lax.broadcasted_iota(I32, (SMAX, width), 0)
    lane_in = lax.broadcasted_iota(I32, (SMAX, width), 1)
    top = row_in == 0
    real_weight, imag_weight = jnp.where(top, 0.5, 1.0), jnp.where(top, 0.0, 1.0)
    edge_weight, flip = jnp.where(top, 1.0, 2.0), jnp.where(lax.rem(row_in, 2) == 0, 1.0, -1.0)
    corner = jnp.where(top & (lax.rem(lane_in, length) == nyquist), 1.0, 0.0)
    quarter = lax.rem(lane_in, 4)
    corner_wave = jnp.where(quarter == 1, -1.0, jnp.where(quarter == 3, 1.0, 0.0))

    def tile(value, t):
        return value[t * SMAX:(t + 1) * SMAX]

    def far_spectra(low, high, stage):
        found = spectra([far_cut(i, stage) for i in range(low, high)])
        for w, value in enumerate(found):
            far_spec[low * chips + w] = value.astype(BF16)

    def far_centres(low, high):
        many = (high - low) * chips
        crossed = []
        for i in range(low, high):
            day = first_s[0, perm_s[0, i] if fast else i]
            for c in range(chips):
                value = far_spec[i * chips + c]
                crossed.append(spec[day * chips + c] * jnp.concatenate([value, value], axis=1))
        reals, imags = [], []
        for start, size in split(many, 1):
            along = jnp.concatenate(crossed[start:start + size], axis=0)
            along = jnp.dot(along, back[...], preferred_element_type=F32)
            for w in range(size):
                part = along[w * kept:(w + 1) * kept]
                reals.append(part[:, :width])
                imags.append(part[:, width:])
        turned = []
        for start, size in split(many, 1):
            both = []
            for w in range(start, start + size):
                last = crossed[w][nyquist:, :width].astype(F32)[:SMAX] * corner
                last = jnp.sum(last, axis=1, keepdims=True) * corner_wave
                last = last + tile(imags[w], tiles)
                imags[w] = jnp.concatenate(
                    [imags[w][:nyquist], last, imags[w][nyquist + SMAX:]], axis=0
                )
                both.append(imags[w].astype(BF16))
            both = jnp.dot(
                final[...], jnp.concatenate(both, axis=1), preferred_element_type=F32
            )
            turned += [both[:, k * width:(k + 1) * width] for k in range(size)]
        for b in range(high - low):
            for c in range(chips):
                w = b * chips + c
                real, imag, turn = reals[w], imags[w], turned[w]
                energy, tilt, nodes = None, None, None
                for t in range(1, tiles):
                    r, i = tile(real, t), tile(imag, t)
                    square = r * r + i * i
                    energy = square if energy is None else energy + square
                    nodes = r if nodes is None else nodes + r
                for t in range(tiles + 1):
                    cross = tile(real, t) * tile(turn, t)
                    tilt = cross if tilt is None else tilt + cross
                r, i = tile(real, 0), tile(imag, 0)
                energy = energy + r * r * real_weight + i * i * imag_weight
                nodes = 2.0 * nodes + r * edge_weight
                r, i = tile(real, tiles), tile(imag, tiles)
                energy = energy + (r * r + i * i) * 0.25
                nodes = jnp.sum((nodes + r) * flip, axis=0, keepdims=True)
                at = (c, pl.ds(low + b, 1))
                sums[at] = jnp.sum(energy, axis=0, keepdims=True) * (2.0 * width)
                tilt = jnp.sum(tilt, axis=0, keepdims=True)
                moments[at] = tilt - nodes * nodes * (0.5 * length)

    def settle(low, high):
        many, cells = high - low, 1.0 / (width * width)
        across = lax.broadcasted_iota(I32, (many, width), 1)
        across = jnp.where(across < length, across, across - width).astype(F32) * 0.5
        some = pl.ds(low, many)
        held_columns, spread, pick = columns_v[some], spread_v[some], picked[some]
        lives = held_columns[:, 2 * chips:2 * chips + 1] > 0.5
        sides, places = [None] * (2 * chips), [None] * (2 * chips)
        for c in range(chips):
            held = sums[c, some]
            scale = jnp.sum(held, axis=1, keepdims=True) * cells + 1e-6
            down_sum = jnp.sum(moments[c, some], axis=1, keepdims=True) * cells
            side_sum = jnp.sum(held * across, axis=1, keepdims=True) * cells
            for x, value in enumerate((down_sum, side_sum)):
                k = x * chips + c
                found = jnp.where(lives, held_columns[:, k:k + 1] + value / scale, 0.0)
                sides[k] = jnp.sum(found * spread, axis=0, keepdims=True)
                places[k] = jnp.sum(found * pick, axis=0, keepdims=True)
        return sides + places

    settled, settled_to = [], 0
    middle = dates // 2
    if fast:
        near_part(0, middle)
        for link, side in ((2, "down"), (4, "up")):
            move.got((link, "now_edge"))
            move.start((6 - link, "relay_edge"))
            move.z_start(side, link)
        move.start((4, "later_rest"), (2, "later_rest"))
        for link, side in ((2, "up"), (4, "down")):
            move.got((link, "later_edge"))
            move.z_start(side, link)
            move.start(("core", link, "edge"))
        near_part(middle, dates)
        for link in (2, 4):
            move.got((link, "now_rest"))
            move.start((6 - link, "relay_rest"), ("core", link, "now"))
        ordered.wait()
        for link, side in ((2, "up"), (4, "down")):
            move.got((link, "relay_edge"))
            move.z_start(side, 6)
            move.start(("core", 6, link, "edge"))
        for k in range(move.inner):
            for link in (2, 4):
                move.got((link, "later_rest", k))
                move.start(("core", link, "rest", k))
        move.got(("core", 0), ("core", 2), ("core", 4))
        for d in (0, 2, 4):
            move.z_got(d)

        def hand_on(*pieces):
            for k in pieces:
                for link in (2, 4):
                    move.got((link, "relay_rest", k))
                    move.start(("core", 6, link, "rest", k))

        early = pairs - 2 * cap
        hand_on(*range(move.inner))
        far_spectra(0, early, 1)
        far_centres(0, early)
        move.got(("core", 6))
        move.z_got(6)
        settled, settled_to = [settle(0, early)], early
        far_spectra(early, pairs, 2)
        far_centres(early, pairs)
        sent = move.kinds
    else:
        near_part(0, middle)
        near_part(middle, dates)
        plain_gather(n, me, strip, strips, grid, send, recv)
        far_spectra(0, pairs, 1)
        far_centres(0, pairs)
        sent = 2 + 3 * (n - 1)

    settled = settled + [settle(settled_to, pairs)]
    joined = [sum(row[1:], row[0]) for row in zip(*settled)]
    for k in range(2 * chips):
        partial[k:k + 1] = joined[k]

    copies = []
    for j in range(1, n):
        where = {"date": lax.rem(me + j, n)}
        copies.append(remote(sent + j - 1, partial, held_sums.at[j - 1], where, send, recv))
        copies[-1].start()
    for x in range(2):
        for c in range(chips):
            offsets_out[x, c:c + 1] = joined[(2 + x) * chips + c]
    if fast:
        move.left()
    total = partial[...]
    for j, copy in enumerate(copies):
        copy.wait_recv()
        total = total + held_sums[j]
    for x in range(2):
        for c in range(chips):
            k = x * chips + c
            value = jnp.sum(inverse[k] * total[k:k + 1], axis=1)[None]
            series_out[x, c:c + 1] = value
    for copy in copies:
        copy.wait_send()


def emit_kernel(offsets, series, offsets_out, series_out, done):
    copies = [
        pltpu.make_async_copy(a, b, done.at[k])
        for k, (a, b) in enumerate(((offsets, offsets_out), (series, series_out)))
    ]
    for copy in copies:
        copy.start()
    for copy in copies:
        copy.wait()


def body(n, strips, images, inverse, first, block, second, count, shifts, anchors):
    dates, length, cols = images.shape
    pairs, chips = first.shape[0], anchors.shape[0]
    vmem, anywhere = pl.BlockSpec(memory_space=pltpu.VMEM), pl.BlockSpec(memory_space=pl.ANY)
    tables = make_tables(length)
    fast = n == 8
    half = length // SMAX // 2
    kinds = (17 + 14 + 8 * PIECES if fast else 2 + 3 * (n - 1)) + n - 1
    width = 2 * length
    cap = 2 * pairs // n
    groups = length // SMAX + 2
    share = inverse.shape[2]
    block_shape = (groups, dates, SMAX, cols)
    late = (2, *block_shape) if fast else (SMAX, cols)
    offsets, series = pl.pallas_call(
        functools.partial(pairs_kernel, n, strips, cap),
        name="pairs",
        out_shape=(
            pltpu.VMEM((2, chips, pairs), F32),
            pltpu.VMEM((2, chips, share), F32),
        ),
        in_specs=[anywhere] * 12,
        out_specs=(vmem, vmem),
        scratch_shapes=[
            pltpu.SMEM((1, pairs), I32),
            pltpu.SMEM((1, pairs), I32),
            pltpu.SMEM((1, pairs), I32),
            pltpu.SMEM((1,), I32),
            pltpu.SMEM((2, chips, pairs), I32),
            pltpu.SMEM((chips,), I32),
            pltpu.SMEM((1, pairs), I32),
            pltpu.VMEM((1, pairs), I32),
            pltpu.VMEM((1, pairs), I32),
            pltpu.VMEM((1, pairs), I32),
            pltpu.VMEM((2, chips, pairs), I32),
            pltpu.VMEM((2 * chips, share, n * dates), F32),
            *[pltpu.VMEM(table.shape, BF16) for table in tables],
            pltpu.VMEM((6 if fast else n, *block_shape), BF16),
            pltpu.VMEM(late, BF16),
            pltpu.VMEM((2 * chips, n * dates), F32),
            pltpu.VMEM((n - 1, 2 * chips, n * dates), F32),
            pltpu.SemaphoreType.DMA((groups + 14,)),
            pltpu.SemaphoreType.DMA((kinds,)),
            pltpu.SemaphoreType.DMA((kinds,)),
            pltpu.VMEM((pairs, length + 2 * SMAX, cols), F32),
            pltpu.VMEM((dates * chips, tables[1].shape[0], 2 * width), BF16),
            pltpu.VMEM((pairs * chips, tables[1].shape[0], width), BF16),
            pltpu.VMEM((chips, pairs, width), F32),
            pltpu.VMEM((chips, pairs, width), F32),
            pltpu.VMEM((pairs, pairs), F32),
            pltpu.VMEM((pairs, n * dates), F32),
            pltpu.VMEM((pairs, cols), F32),
            pltpu.VMEM((1, pairs), I32),
        ],
        compiler_params=pltpu.CompilerParams(collective_id=0, has_side_effects=True),
    )(
        first.reshape(1, pairs), block.reshape(1, pairs), second.reshape(1, pairs), count,
        jnp.transpose(shifts, (1, 2, 0)), anchors,
        images.reshape(dates, length // SMAX, SMAX, cols),
        inverse.reshape(2 * chips, share, n * dates), *tables,
    )
    offsets, series = pl.pallas_call(
        emit_kernel,
        name="emit",
        out_shape=(
            jax.ShapeDtypeStruct(offsets.shape, F32),
            jax.ShapeDtypeStruct(series.shape, F32),
        ),
        in_specs=[vmem] * 2,
        out_specs=(anywhere, anywhere),
        scratch_shapes=[pltpu.SemaphoreType.DMA((2,))],
    )(
        pltpu.with_memory_space_constraint(offsets, pltpu.VMEM),
        pltpu.with_memory_space_constraint(series, pltpu.VMEM),
    )
    return jnp.transpose(offsets, (2, 0, 1)), series


def solution(mesh):
    return jax.shard_map(
        functools.partial(body, mesh.shape["date"], mesh.shape["strip"]),
        mesh=mesh,
        in_specs=(
            P("date", "strip", None),
            P(None, "strip", "date", None),
            P("date"),
            P("date", None),
            P("date"),
            P("date"),
            P("date", None, "strip"),
            P("strip"),
        ),
        out_specs=(P("date", None, "strip"), P(None, "strip", "date")),
        check_vma=False,
    )
```

```python
import functools
import math

import jax
import jax.numpy as jnp
import numpy as np
from jax import lax
from jax.experimental import pallas as pl
from jax.experimental.pallas import tpu as pltpu
from jax.sharding import PartitionSpec as P

SMAX = 8
SPLIT = 8
PIECES = 1
MESH = pl.DeviceIdType.MESH
F32, BF16, I32 = jnp.float32, jnp.bfloat16, jnp.int32


def make_tables(length):
    counter = np.arange(length)
    radians = (counter[:, None] * counter[None, :] % length) * (2.0 * math.pi / length)
    cosine, sine = np.cos(radians), -np.sin(radians)
    over = 2 * length
    signed = np.where(counter < length // 2, counter, counter - length)
    places = np.arange(over)
    angles = (signed[:, None] * places[None, :] % over) * (2.0 * math.pi / over)
    vcos, vsin = np.cos(angles), np.sin(angles)
    forward = np.concatenate([cosine, sine], axis=1)
    empty = np.zeros_like(forward)
    forward = np.block([[forward, empty], [empty, forward]])
    half = length // 2
    kept = -(-(half + 1) // 16) * 16
    rows = np.zeros((kept, over))
    rows[:half + 1] = np.concatenate([cosine, sine], axis=1)[:half + 1]
    vsin[half] = 0.0
    one = np.concatenate([vcos, vsin], axis=1)
    two = np.concatenate([-vsin, vcos], axis=1)
    back = np.concatenate([one, one, two, -two], axis=0)
    lean = ((places + length) % over - length) * 0.5
    waves = counter[:half + 1, None] * places[None, :] * (2.0 * math.pi / over)
    even = np.where((counter[:half + 1] == 0) | (counter[:half + 1] == half), 1.0, 2.0)
    odd = np.where(counter[:half + 1] == half, 1.0, -2.0)
    final = np.zeros((kept, kept))
    final[:half + 1, :half + 1] = 2.0 * (even[:, None] * np.cos(waves) * lean) @ (
        odd[:, None] * np.sin(waves)
    ).T
    return [jnp.asarray(t.astype(np.float32)).astype(BF16) for t in (forward, rows, back, final)]


def remote(k, src, dst, where, send, recv):
    return pltpu.make_async_remote_copy(
        src_ref=src,
        dst_ref=dst,
        send_sem=send.at[k],
        recv_sem=recv.at[k],
        device_id=where,
        device_id_type=MESH,
    )


class Gather:
    def __init__(self, me, strip, strips, blocks, send, recv):
        self.blocks = blocks
        groups = blocks[0].shape[0]
        half = (groups - 2) // 2
        last = groups - 2
        self.has_up, self.has_down = strip > 0, strip < strips - 1
        up, down = lax.max(strip - 1, 0), lax.min(strip + 1, strips - 1)
        to = {j: jnp.bitwise_xor(me, j) for j in (1, 2, 4)}
        self.to, self.up, self.down = to, up, down
        self.copies = {}
        self.kinds = 0

        def add(name, d, at, many, where, target, dst_at=None):
            dst_at = at if dst_at is None else dst_at
            copy = remote(
                self.kinds,
                blocks[d].at[pl.ds(at, many)],
                blocks[target].at[pl.ds(dst_at, many)],
                where,
                send,
                recv,
            )
            self.copies[name] = copy
            self.kinds += 1

        edges = {"one": 1, "two": last}
        rests = {"one": 2, "two": 1 + half}
        inner = half - 1
        core = {"date": to[1]}
        add(("core", 0), 0, 1, 2 * half, core, 1)
        for link, now, later, relayed in ((4, "one", "two", 2), (2, "two", "one", 4)):
            where = {"date": to[link]}
            add((link, "now_edge"), 0, edges[now], 1, where, link)
            add((link, "now_rest"), 0, rests[now], inner, where, link)
            add((link, "later_edge"), 0, edges[later], 1, where, link)
            add((link, "relay_edge"), relayed, edges[later], 1, where, 6)
            begin = min(edges[now], rests[now])
            add(("core", link, "now"), link, begin, half, core, link ^ 1)
            add(("core", link, "edge"), link, edges[later], 1, core, link ^ 1)
            add(("core", 6, link, "edge"), 6, edges[later], 1, core, 7)
            for k in range(PIECES):
                many = inner // PIECES
                at = rests[later] + k * many
                add((link, "later_rest", k), 0, at, many, where, link)
                add((link, "relay_rest", k), relayed, at, many, where, 6)
                add(("core", link, "rest", k), link, at, many, core, link ^ 1)
                add(("core", 6, link, "rest", k), 6, at, many, core, 7)
        self.inner = PIECES
        for d in (0, 2, 4, 6):
            for flip in (0, 1):
                spot = {"date": jnp.bitwise_xor(me, flip)} if flip else {}
                add(("up", d, flip), d, 1, 1, {"strip": up, **spot}, d ^ flip, groups - 1)
                add(("down", d, flip), d, last, 1, {"strip": down, **spot}, d ^ flip, 0)

    def named(self, names):
        for key, copy in self.copies.items():
            if key in names or key[:2] in names:
                yield copy

    def start(self, *names):
        for copy in self.named(names):
            copy.start()

    def got(self, *names):
        for copy in self.named(names):
            copy.wait_recv()

    def z_start(self, side, d):
        has = self.has_up if side == "up" else self.has_down

        @pl.when(has)
        def _():
            for flip in (0, 1):
                self.copies[(side, d, flip)].start()

    def z_got(self, d, flips=(0, 1)):
        @pl.when(self.has_down)
        def _():
            for flip in flips:
                self.copies[("up", d, flip)].wait_recv()

        @pl.when(self.has_up)
        def _():
            for flip in flips:
                self.copies[("down", d, flip)].wait_recv()

    def left(self):
        for name, copy in self.copies.items():
            if name[0] == "up":
                pl.when(self.has_up)(copy.wait_send)
            elif name[0] == "down":
                pl.when(self.has_down)(copy.wait_send)
            else:
                copy.wait_send()


def plain_gather(n, me, strip, strips, grid, send, recv):
    groups = grid.shape[1]
    has_up, has_down = strip > 0, strip < strips - 1
    up, down = lax.max(strip - 1, 0), lax.min(strip + 1, strips - 1)
    z_up = remote(0, grid.at[me, 1], grid.at[me, groups - 1], {"strip": up}, send, recv)
    z_down = remote(1, grid.at[me, groups - 2], grid.at[me, 0], {"strip": down}, send, recv)
    pl.when(has_up)(z_up.start)
    pl.when(has_down)(z_down.start)
    copies = []
    peers = [{"date": lax.rem(me + j, n)} for j in range(1, n)]
    main = pl.ds(1, groups - 2)
    for j, peer in enumerate(peers):
        part = grid.at[me, main]
        copies.append(remote(2 + j, part, part, peer, send, recv))
        copies[-1].start()
    pl.when(has_down)(z_up.wait_recv)
    pl.when(has_up)(z_down.wait_recv)
    pl.when(has_up)(z_up.wait_send)
    pl.when(has_down)(z_down.wait_send)
    for side, at in ((0, 0), (1, groups - 1)):
        for j, peer in enumerate(peers):
            part = grid.at[me, at]
            copies.append(remote(2 + (1 + side) * (n - 1) + j, part, part, peer, send, recv))
            copies[-1].start()
    for copy in copies:
        copy.wait()


def pairs_kernel(
    n, strips, cap,
    first_h, block_h, second_h, count_h, shifts_h, anchors_h,
    img, inverse_h, forward_h, rows_h, back_h, final_h,
    offsets_out, series_out,
    first_s, block_s, second_s, count_s, shifts_s, anchors_s, perm_s,
    first_v, block_v, second_v, shifts_v, inverse, forward, rows, back, final,
    grid, late, partial, held_sums,
    local, send, recv,
    wide, spec, far_spec, sums, moments, picked, spread_v, columns_v, perm_v,
):
    groups, dates, _, cols = grid.shape[1:]
    length = SMAX * (groups - 2)
    pairs, chips = first_s.shape[1], anchors_s.shape[0]
    fast = n == 8
    me, strip = lax.axis_index("date"), lax.axis_index("strip")
    has_up, has_down = strip > 0, strip < strips - 1
    up, down = lax.max(strip - 1, 0), lax.min(strip + 1, strips - 1)

    barrier = pltpu.get_barrier_semaphore()
    if fast:
        greeted = [{"date": jnp.bitwise_xor(me, j)} for j in (1, 2, 4)]
        side_spots = [{}, {"date": jnp.bitwise_xor(me, 1)}]
    else:
        greeted = [{"date": lax.rem(me + j, n)} for j in range(1, n)]
        side_spots = [{}]
    for where in greeted:
        pl.semaphore_signal(barrier, inc=1, device_id=where, device_id_type=MESH)
    for other, has in ((up, has_up), (down, has_down)):
        @pl.when(has)
        def _():
            for spot in side_spots:
                pl.semaphore_signal(
                    barrier, inc=1, device_id={"strip": other, **spot}, device_id_type=MESH
                )

    count = iter(range(local.shape[0]))

    def load(src, dst):
        copy = pltpu.make_async_copy(src, dst, local.at[next(count)])
        copy.start()
        return copy

    own = 0 if fast else me
    spots = [0, groups - 3, *range(1, groups - 3)]
    mine = [load(img.at[:, g], grid.at[own, 1 + g]) for g in spots]
    sides = len(side_spots) * (has_up.astype(I32) + has_down.astype(I32))
    pl.semaphore_wait(barrier, len(greeted) + sides)
    for copy in mine[:2]:
        copy.wait()
    if fast:
        blocks = [grid.at[d] for d in range(6)] + [late.at[d] for d in range(2)]
        move = Gather(me, strip, strips, blocks, send, recv)
        move.start((4, "now_edge"), (2, "now_edge"))
        move.start((4, "later_edge"), (2, "later_edge"))
        move.z_start("up", 0)
        move.z_start("down", 0)
    small = [
        load(a, b)
        for a, b in (
            (first_h, first_s), (block_h, block_s), (second_h, second_s), (count_h, count_s),
            (shifts_h, shifts_s), (anchors_h, anchors_s),
            (first_h, first_v), (block_h, block_v), (second_h, second_v), (shifts_h, shifts_v),
        )
    ]
    large = [
        load(a, b)
        for a, b in (
            (forward_h, forward), (rows_h, rows), (back_h, back), (final_h, final),
            (inverse_h, inverse),
        )
    ]
    for copy in mine[2:]:
        copy.wait()
    if fast:
        move.start((4, "now_rest"), (2, "now_rest"), ("core", 0))
    for copy in small + large:
        copy.wait()

    line = lax.broadcasted_iota(I32, (pairs, pairs), 0)
    place = lax.broadcasted_iota(I32, (pairs, pairs), 1)
    if fast:
        distance = jnp.bitwise_xor(block_v[...], me)
        key = jnp.broadcast_to(jnp.maximum(distance - 5, 0), (pairs, pairs))
        key_line = jnp.sum(jnp.where(line == place, key, 0), axis=1, keepdims=True)
        ahead = (key < key_line) | ((key == key_line) & (place < line))
        rank_line = jnp.sum(ahead.astype(I32), axis=1, keepdims=True)
        behind = (key_line < key) | ((key_line == key) & (line < place))
        rank = jnp.sum(behind.astype(I32), axis=0, keepdims=True)
        perm_v[...] = jnp.sum(jnp.where(rank_line == place, line, 0), axis=0, keepdims=True)
        ordered = load(perm_v, perm_s)
        pick = (jnp.broadcast_to(rank, (pairs, pairs)) == line).astype(F32)
    else:
        pick = (line == place).astype(F32)
    picked[...] = pick

    def chosen(row):
        return jnp.sum(pick * row, axis=1, keepdims=True)

    spot = lax.broadcasted_iota(I32, (pairs, partial.shape[1]), 1).astype(F32)
    to_date = chosen((block_v[...] * dates + second_v[...]).astype(F32))
    from_date = chosen((me * dates + first_v[...]).astype(F32))
    spread_v[...] = (spot == to_date).astype(F32) - (spot == from_date).astype(F32)
    live = (lax.broadcasted_iota(I32, (1, pairs), 1) < count_s[0]).astype(F32)
    at = lax.broadcasted_iota(I32, columns_v.shape, 1)
    held_columns = jnp.where(at == 2 * chips, chosen(live), 0.0)
    for x in range(2):
        for c in range(chips):
            column = chosen(shifts_v[x, c:c + 1].astype(F32))
            held_columns = jnp.where(at == x * chips + c, column, held_columns)
    columns_v[...] = held_columns

    lane = lax.broadcasted_iota(I32, (1, cols), 1)
    left_half = lane < length

    def paired(one, start_one, two, start_two):
        one = pltpu.roll(one.astype(BF16), lax.rem(2 * cols - start_one, cols), 1)
        two = pltpu.roll(two.astype(BF16), lax.rem(2 * cols + length - start_two, cols), 1)
        column = jnp.where(left_half, start_one + lane, start_two - length + lane)
        inside = (column >= 0) & (column < cols)
        keep_one = jnp.where(left_half & inside, 1.0, 0.0).astype(BF16)
        keep_two = jnp.where(left_half, 0.0, jnp.where(inside, 1.0, 0.0)).astype(BF16)
        return one * keep_one + two * keep_two

    width = 2 * length
    lanes2 = lax.broadcasted_iota(I32, (1, 2 * width), 1)
    base = jnp.where((lanes2 == 0) | (lanes2 == width), 1.0 / length, 0.0)
    turn_sign = jnp.where(left_half, -1.0, 1.0).astype(BF16)

    def split(many, size):
        step = max(1, many // SPLIT) * size
        return [(at, step) for at in range(0, many * size, step)]

    def spectra(windows):
        many = len(windows)
        sections = []
        for start, size in split(many, length):
            some = windows[start // length:(start + size) // length]
            found = jnp.dot(
                jnp.concatenate(some, axis=0), forward[...], preferred_element_type=F32
            )
            sections += [found[k:k + length] for k in range(0, size, length)]
        stacked = []
        for part in sections:
            part = part - jnp.sum(part, axis=0, keepdims=True) * base
            for c in range(2):
                top = part[:, c * width:(c + 1) * width]
                top = top.astype(BF16)
                low = pltpu.roll(top, length, 1) * turn_sign
                stacked.append(jnp.concatenate([top, low], axis=0))
        found = []
        for start, size in split(many, 2):
            both = jnp.concatenate(stacked[start:start + size], axis=1)
            both = jnp.dot(rows[...], both, preferred_element_type=F32)
            found += [both[:, k * width:(k + 1) * width] for k in range(size)]
        return found

    def near_part(low, high):
        windows = []
        for d in range(low, high):
            value = grid[own, pl.ds(1, groups - 2), d].astype(F32).reshape(length, cols)
            windows.append(paired(value, anchors_s[0], value, anchors_s[1]))
        found = spectra(windows)
        for w in range((high - low) * chips):
            both = jnp.concatenate([found[w], pltpu.roll(found[w], length, 1)], axis=1)
            spec[low * chips + w] = both.astype(BF16)

    def far_cut(i, stage):
        p = perm_s[0, i] if fast else i
        block, day = block_s[0, p], second_s[0, p]
        if fast:
            distance = jnp.bitwise_xor(block, me)
            value = grid[jnp.where(distance < 6, distance, 0), :, day]
            if stage > 1:
                other = late[jnp.where(distance == 7, 1, 0), :, day]
                value = jnp.where(distance < 6, value, other)
            value = value.astype(F32)
        else:
            value = grid[block, :, day].astype(F32)
        wide[i, pl.ds(0, SMAX)] = jnp.where(has_up, value[0], 0.0)
        wide[i, pl.ds(SMAX, length)] = value[1:groups - 1].reshape(length, cols)
        wide[i, pl.ds(SMAX + length, SMAX)] = jnp.where(has_down, value[groups - 1], 0.0)
        windows = []
        for c in range(2):
            windows.append(wide[i, pl.ds(SMAX + shifts_s[0, c, p], length)])
            windows.append(anchors_s[c] + shifts_s[1, c, p])
        return paired(*windows)

    kept, nyquist = rows.shape[0], length // 2
    tiles = nyquist // SMAX
    row_in = lax.broadcasted_iota(I32, (SMAX, width), 0)
    lane_in = lax.broadcasted_iota(I32, (SMAX, width), 1)
    top = row_in == 0
    real_weight, imag_weight = jnp.where(top, 0.5, 1.0), jnp.where(top, 0.0, 1.0)
    edge_weight, flip = jnp.where(top, 1.0, 2.0), jnp.where(lax.rem(row_in, 2) == 0, 1.0, -1.0)
    corner = jnp.where(top & (lax.rem(lane_in, length) == nyquist), 1.0, 0.0)
    quarter = lax.rem(lane_in, 4)
    corner_wave = jnp.where(quarter == 1, -1.0, jnp.where(quarter == 3, 1.0, 0.0))

    def tile(value, t):
        return value[t * SMAX:(t + 1) * SMAX]

    def far_spectra(low, high, stage):
        found = spectra([far_cut(i, stage) for i in range(low, high)])
        for w, value in enumerate(found):
            far_spec[low * chips + w] = value.astype(BF16)

    def far_centres(low, high):
        many = (high - low) * chips
        crossed = []
        for i in range(low, high):
            day = first_s[0, perm_s[0, i] if fast else i]
            for c in range(chips):
                value = far_spec[i * chips + c]
                crossed.append(spec[day * chips + c] * jnp.concatenate([value, value], axis=1))
        reals, imags = [], []
        for start, size in split(many, 1):
            along = jnp.concatenate(crossed[start:start + size], axis=0)
            along = jnp.dot(along, back[...], preferred_element_type=F32)
            for w in range(size):
                part = along[w * kept:(w + 1) * kept]
                reals.append(part[:, :width])
                imags.append(part[:, width:])
        turned = []
        for start, size in split(many, 1):
            both = []
            for w in range(start, start + size):
                last = crossed[w][nyquist:, :width].astype(F32)[:SMAX] * corner
                last = jnp.sum(last, axis=1, keepdims=True) * corner_wave
                last = last + tile(imags[w], tiles)
                imags[w] = jnp.concatenate(
                    [imags[w][:nyquist], last, imags[w][nyquist + SMAX:]], axis=0
                )
                both.append(imags[w].astype(BF16))
            both = jnp.dot(
                final[...], jnp.concatenate(both, axis=1), preferred_element_type=F32
            )
            turned += [both[:, k * width:(k + 1) * width] for k in range(size)]
        for b in range(high - low):
            for c in range(chips):
                w = b * chips + c
                real, imag, turn = reals[w], imags[w], turned[w]
                energy, tilt, nodes = None, None, None
                for t in range(1, tiles):
                    r, i = tile(real, t), tile(imag, t)
                    square = r * r + i * i
                    energy = square if energy is None else energy + square
                    nodes = r if nodes is None else nodes + r
                for t in range(tiles + 1):
                    cross = tile(real, t) * tile(turn, t)
                    tilt = cross if tilt is None else tilt + cross
                r, i = tile(real, 0), tile(imag, 0)
                energy = energy + r * r * real_weight + i * i * imag_weight
                nodes = 2.0 * nodes + r * edge_weight
                r, i = tile(real, tiles), tile(imag, tiles)
                energy = energy + (r * r + i * i) * 0.25
                nodes = jnp.sum((nodes + r) * flip, axis=0, keepdims=True)
                at = (c, pl.ds(low + b, 1))
                sums[at] = jnp.sum(energy, axis=0, keepdims=True) * (2.0 * width)
                tilt = jnp.sum(tilt, axis=0, keepdims=True)
                moments[at] = tilt - nodes * nodes * (0.5 * length)

    def settle(low, high):
        many, cells = high - low, 1.0 / (width * width)
        across = lax.broadcasted_iota(I32, (many, width), 1)
        across = jnp.where(across < length, across, across - width).astype(F32) * 0.5
        some = pl.ds(low, many)
        held_columns, spread, pick = columns_v[some], spread_v[some], picked[some]
        lives = held_columns[:, 2 * chips:2 * chips + 1] > 0.5
        sides, places = [None] * (2 * chips), [None] * (2 * chips)
        for c in range(chips):
            held = sums[c, some]
            scale = jnp.sum(held, axis=1, keepdims=True) * cells + 1e-6
            down_sum = jnp.sum(moments[c, some], axis=1, keepdims=True) * cells
            side_sum = jnp.sum(held * across, axis=1, keepdims=True) * cells
            for x, value in enumerate((down_sum, side_sum)):
                k = x * chips + c
                found = jnp.where(lives, held_columns[:, k:k + 1] + value / scale, 0.0)
                sides[k] = jnp.sum(found * spread, axis=0, keepdims=True)
                places[k] = jnp.sum(found * pick, axis=0, keepdims=True)
        return sides + places

    settled, settled_to = [], 0
    middle = dates // 2
    if fast:
        near_part(0, middle)
        for link, side in ((2, "down"), (4, "up")):
            move.got((link, "now_edge"))
            move.start((6 - link, "relay_edge"))
            move.z_start(side, link)
        move.start((4, "later_rest"), (2, "later_rest"))
        for link, side in ((2, "up"), (4, "down")):
            move.got((link, "later_edge"))
            move.z_start(side, link)
            move.start(("core", link, "edge"))
        near_part(middle, dates)
        for link in (2, 4):
            move.got((link, "now_rest"))
            move.start((6 - link, "relay_rest"), ("core", link, "now"))
        ordered.wait()
        for link, side in ((2, "up"), (4, "down")):
            move.got((link, "relay_edge"))
            move.z_start(side, 6)
            move.start(("core", 6, link, "edge"))
        for k in range(move.inner):
            for link in (2, 4):
                move.got((link, "later_rest", k))
                move.start(("core", link, "rest", k))
        move.got(("core", 0), ("core", 2), ("core", 4))
        for d in (0, 2, 4):
            move.z_got(d)

        def hand_on(*pieces):
            for k in pieces:
                for link in (2, 4):
                    move.got((link, "relay_rest", k))
                    move.start(("core", 6, link, "rest", k))

        early = pairs - 2 * cap
        hand_on(*range(move.inner))
        far_spectra(0, early, 1)
        far_centres(0, early)
        move.got(("core", 6))
        move.z_got(6)
        settled, settled_to = [settle(0, early)], early
        far_spectra(early, pairs, 2)
        far_centres(early, pairs)
        sent = move.kinds
    else:
        near_part(0, middle)
        near_part(middle, dates)
        plain_gather(n, me, strip, strips, grid, send, recv)
        far_spectra(0, pairs, 1)
        far_centres(0, pairs)
        sent = 2 + 3 * (n - 1)

    settled = settled + [settle(settled_to, pairs)]
    joined = [sum(row[1:], row[0]) for row in zip(*settled)]
    for k in range(2 * chips):
        partial[k:k + 1] = joined[k]

    copies = []
    for j in range(1, n):
        where = {"date": lax.rem(me + j, n)}
        copies.append(remote(sent + j - 1, partial, held_sums.at[j - 1], where, send, recv))
        copies[-1].start()
    for x in range(2):
        for c in range(chips):
            offsets_out[x, c:c + 1] = joined[(2 + x) * chips + c]
    if fast:
        move.left()
    total = partial[...]
    for j, copy in enumerate(copies):
        copy.wait_recv()
        total = total + held_sums[j]
    for x in range(2):
        for c in range(chips):
            k = x * chips + c
            value = jnp.sum(inverse[k] * total[k:k + 1], axis=1)[None]
            series_out[x, c:c + 1] = value
    for copy in copies:
        copy.wait_send()


def emit_kernel(offsets, series, offsets_out, series_out, done):
    copies = [
        pltpu.make_async_copy(a, b, done.at[k])
        for k, (a, b) in enumerate(((offsets, offsets_out), (series, series_out)))
    ]
    for copy in copies:
        copy.start()
    for copy in copies:
        copy.wait()


def body(n, strips, images, inverse, first, block, second, count, shifts, anchors):
    dates, length, cols = images.shape
    pairs, chips = first.shape[0], anchors.shape[0]
    vmem, anywhere = pl.BlockSpec(memory_space=pltpu.VMEM), pl.BlockSpec(memory_space=pl.ANY)
    tables = make_tables(length)
    fast = n == 8
    half = length // SMAX // 2
    kinds = (17 + 14 + 8 * PIECES if fast else 2 + 3 * (n - 1)) + n - 1
    width = 2 * length
    cap = 2 * pairs // n
    groups = length // SMAX + 2
    share = inverse.shape[2]
    block_shape = (groups, dates, SMAX, cols)
    late = (2, *block_shape) if fast else (SMAX, cols)
    offsets, series = pl.pallas_call(
        functools.partial(pairs_kernel, n, strips, cap),
        name="pairs",
        out_shape=(
            pltpu.VMEM((2, chips, pairs), F32),
            pltpu.VMEM((2, chips, share), F32),
        ),
        in_specs=[anywhere] * 12,
        out_specs=(vmem, vmem),
        scratch_shapes=[
            pltpu.SMEM((1, pairs), I32),
            pltpu.SMEM((1, pairs), I32),
            pltpu.SMEM((1, pairs), I32),
            pltpu.SMEM((1,), I32),
            pltpu.SMEM((2, chips, pairs), I32),
            pltpu.SMEM((chips,), I32),
            pltpu.SMEM((1, pairs), I32),
            pltpu.VMEM((1, pairs), I32),
            pltpu.VMEM((1, pairs), I32),
            pltpu.VMEM((1, pairs), I32),
            pltpu.VMEM((2, chips, pairs), I32),
            pltpu.VMEM((2 * chips, share, n * dates), F32),
            *[pltpu.VMEM(table.shape, BF16) for table in tables],
            pltpu.VMEM((6 if fast else n, *block_shape), BF16),
            pltpu.VMEM(late, BF16),
            pltpu.VMEM((2 * chips, n * dates), F32),
            pltpu.VMEM((n - 1, 2 * chips, n * dates), F32),
            pltpu.SemaphoreType.DMA((groups + 14,)),
            pltpu.SemaphoreType.DMA((kinds,)),
            pltpu.SemaphoreType.DMA((kinds,)),
            pltpu.VMEM((pairs, length + 2 * SMAX, cols), F32),
            pltpu.VMEM((dates * chips, tables[1].shape[0], 2 * width), BF16),
            pltpu.VMEM((pairs * chips, tables[1].shape[0], width), BF16),
            pltpu.VMEM((chips, pairs, width), F32),
            pltpu.VMEM((chips, pairs, width), F32),
            pltpu.VMEM((pairs, pairs), F32),
            pltpu.VMEM((pairs, n * dates), F32),
            pltpu.VMEM((pairs, cols), F32),
            pltpu.VMEM((1, pairs), I32),
        ],
        compiler_params=pltpu.CompilerParams(collective_id=0, has_side_effects=True),
    )(
        first.reshape(1, pairs), block.reshape(1, pairs), second.reshape(1, pairs), count,
        jnp.transpose(shifts, (1, 2, 0)), anchors,
        images.reshape(dates, length // SMAX, SMAX, cols),
        inverse.reshape(2 * chips, share, n * dates), *tables,
    )
    offsets, series = pl.pallas_call(
        emit_kernel,
        name="emit",
        out_shape=(
            jax.ShapeDtypeStruct(offsets.shape, F32),
            jax.ShapeDtypeStruct(series.shape, F32),
        ),
        in_specs=[vmem] * 2,
        out_specs=(anywhere, anywhere),
        scratch_shapes=[pltpu.SemaphoreType.DMA((2,))],
    )(
        pltpu.with_memory_space_constraint(offsets, pltpu.VMEM),
        pltpu.with_memory_space_constraint(series, pltpu.VMEM),
    )
    return jnp.transpose(offsets, (2, 0, 1)), series


def solution(mesh):
    return jax.shard_map(
        functools.partial(body, mesh.shape["date"], mesh.shape["strip"]),
        mesh=mesh,
        in_specs=(
            P("date", "strip", None),
            P(None, "strip", "date", None),
            P("date"),
            P("date", None),
            P("date"),
            P("date"),
            P("date", None, "strip"),
            P("strip"),
        ),
        out_specs=(P("date", None, "strip"), P(None, "strip", "date")),
        check_vma=False,
    )
```
